256 devices in a mesh: grp: 16 (over y_lo, z), seq: 16 (over y_hi, x, core).
Axes of the slice: x: 4, y: 4 (y_hi: 2, y_lo: 2; y = y_hi * 2 + y_lo), z: 8, core: 2. Of those that a mesh axis runs over, the one named last changes fastest.
Arguments:
- query_rows: bfloat16 [131072, 1024], P(('grp', 'seq')), may hold values from -96 to 96
- key_rows: bfloat16 [131072, 1024], P(('grp', 'seq')), may hold values from -8 to 8
- value_rows: bfloat16 [131072, 1024], P(('grp', 'seq')), may hold values from -12 to 12
- grad_out: bfloat16 [131072, 1024], P(('grp', 'seq')), may hold values from -6 to 6
Outputs:
- attended: bfloat16 [131072, 1024], P(('grp', 'seq'))
- grad_query: bfloat16 [131072, 1024], P(('grp', 'seq'))
- grad_key: bfloat16 [131072, 1024], P(('grp', 'seq'))
- grad_value: bfloat16 [131072, 1024], P(('grp', 'seq'))
The draws below stay inside these ranges and needn't reach their ends.
All inputs are finite; a program needn't handle non-finite values.
Results may differ from the reference program's by a relative error of at most 0.0051.
Values may be sent and summed in bfloat16 or wider, within the bound.
A program may use at most 128 MiB of HBM per device.

```python
import jax
import jax.numpy as jnp
from jax import lax

HEADS = 8
HEAD_DIM = 128
BLOCK = 512
NEAR = 256
POOL1 = 16
MERGE = 16
WIDTH = 1024
SEQ = 131072
N_GRP = 16
N_SEQ = 16


def region_part(key, scale):
    regions = SEQ // (POOL1 * MERGE)
    common = jnp.clip(jax.random.normal(key, (regions, WIDTH), jnp.float32), -3.0, 3.0) * scale
    spread = jnp.broadcast_to(common[:, None, :], (regions, POOL1 * MERGE, WIDTH))
    return spread.reshape(SEQ, WIDTH)


def key_floats(key):
    first, second = jax.random.split(jax.random.fold_in(key, 202), 2)
    rough = jnp.clip(jax.random.normal(first, (SEQ, WIDTH), jnp.float32), -4.0, 4.0)
    keys_all = rough + region_part(second, 1.0)
    return jnp.clip(keys_all, -8.0, 8.0)


def draw_key_rows(key, part):
    return key_floats(key).astype(jnp.bfloat16)


def draw_query_rows(key, part):
    first = jax.random.fold_in(jax.random.fold_in(key, 303), 0)
    base = 1.5 * jnp.clip(jax.random.normal(first, (SEQ, WIDTH), jnp.float32), -4.0, 4.0)
    return jnp.clip(base, -96.0, 96.0).astype(jnp.bfloat16)


def draw_value_rows(key, part):
    first, second = jax.random.split(jax.random.fold_in(key, 404))
    rough = jnp.clip(jax.random.normal(first, (SEQ, WIDTH), jnp.float32), -4.0, 4.0)
    values = rough + region_part(second, 1.5)
    return jnp.clip(values, -12.0, 12.0).astype(jnp.bfloat16)


def block_scale(rng, extent, pieces, least, high):
    def one(dim, blocks):
        draws = jax.random.uniform(jax.random.fold_in(jax.random.fold_in(rng, 6), dim), (blocks,), jnp.float32, least / len(pieces), high / len(pieces))
        return jnp.repeat(jnp.exp(draws), extent[dim] // blocks).reshape((-1,) + (1,) * (len(extent) - dim - 1))

    loudness = one(*pieces[0])
    for cut in pieces[1:]:
        loudness = loudness * one(*cut)
    return loudness


def normal_values(key, dims, width, bound, shards=(), kind=jnp.bfloat16):
    array = jax.random.normal(key, dims, jnp.float32) * width
    if len(shards) > 0:
        array = block_scale(key, dims, shards, -0.22, 0.18) * array
    return jnp.clip(array, min=-bound, max=bound).astype(kind)


def setup_inputs(seed: int = 0) -> dict:
    keys = jax.random.split(jax.random.key(seed), 5)
    return {
        "query_rows": draw_query_rows(jax.random.fold_in(keys[4], 71), 0),
        "key_rows": draw_key_rows(jax.random.fold_in(keys[4], 71), 0),
        "value_rows": draw_value_rows(jax.random.fold_in(keys[4], 71), 0),
        "grad_out": normal_values(keys[3], (SEQ, WIDTH), 1.0, 6.0, ((0, 256),)),
    }


NEG_FILL = -1.0e30


def pool_rows(values, factor):
    groups = values.shape[-2] // factor
    shaped = values.reshape(values.shape[:-2] + (groups, factor, values.shape[-1]))
    return jnp.mean(shaped, axis=-2, dtype=jnp.float32)


def expand_rows(values, factor):
    spread = jnp.broadcast_to(values[..., :, None, :], values.shape[:-1] + (factor, values.shape[-1]))
    return spread.reshape(values.shape[:-2] + (values.shape[-2] * factor, values.shape[-1]))


def attend_block(query_block, grad_block, key_set, value_set, bias_row):
    scaling = HEAD_DIM ** -0.5
    queries = query_block.reshape(BLOCK, HEADS, HEAD_DIM).astype(jnp.float32)
    grad_heads = grad_block.reshape(BLOCK, HEADS, HEAD_DIM).astype(jnp.float32)
    key_heads = key_set.reshape(-1, HEADS, HEAD_DIM).astype(jnp.float32)
    value_heads = value_set.reshape(-1, HEADS, HEAD_DIM).astype(jnp.float32)
    scores = jnp.einsum("qhd,khd->hqk", queries, key_heads) * scaling + bias_row
    weights = jax.nn.softmax(scores, axis=-1)
    rounded = lax.optimization_barrier(weights.astype(jnp.bfloat16)).astype(jnp.float32)
    attended = jnp.einsum("hqk,khd->qhd", rounded, value_heads).reshape(BLOCK, WIDTH).astype(jnp.bfloat16)
    weight_grads = jnp.einsum("qhd,khd->hqk", grad_heads, value_heads)
    centre = jnp.sum(weights * weight_grads, axis=-1, keepdims=True)
    score_grads = lax.optimization_barrier((weights * (weight_grads - centre)).astype(jnp.bfloat16)).astype(jnp.float32)
    grad_query = (jnp.einsum("hqk,khd->qhd", score_grads, key_heads) * scaling).reshape(BLOCK, WIDTH).astype(jnp.bfloat16)
    key_grads = (jnp.einsum("hqk,qhd->khd", score_grads, queries) * scaling).reshape(-1, WIDTH)
    value_grads = jnp.einsum("hqk,qhd->khd", rounded, grad_heads).reshape(-1, WIDTH)
    return attended, grad_query, key_grads, value_grads


def add_rows(total, update, start):
    current = lax.dynamic_slice_in_dim(total, start, update.shape[0])
    return lax.dynamic_update_slice_in_dim(total, current + update, start, 0)


def reference(query_rows, key_rows, value_rows, grad_out):
    blocks = N_GRP * N_SEQ
    rows_one = BLOCK // POOL1
    rows_two = rows_one // MERGE
    group_rows = N_SEQ * rows_one
    band = BLOCK + 2 * NEAR
    total_tokens = blocks * BLOCK
    pooled_key = pool_rows(key_rows.astype(jnp.float32), POOL1).astype(jnp.bfloat16)
    pooled_value = pool_rows(value_rows.astype(jnp.float32), POOL1).astype(jnp.bfloat16)
    coarse_key = pool_rows(pooled_key.astype(jnp.float32), MERGE).astype(jnp.bfloat16)
    coarse_value = pool_rows(pooled_value.astype(jnp.float32), MERGE).astype(jnp.bfloat16)
    margin = jnp.zeros((NEAR, WIDTH), jnp.bfloat16)
    padded_key = jnp.concatenate([margin, key_rows, margin], axis=0)
    padded_value = jnp.concatenate([margin, value_rows, margin], axis=0)
    band_offsets = jnp.arange(band, dtype=jnp.int32) - NEAR
    pool_block = jnp.arange(group_rows, dtype=jnp.int32) // rows_one
    coarse_group = jnp.arange(blocks * rows_two, dtype=jnp.int32) // (N_SEQ * rows_two)

    def visit(carry, block_index):
        key_band, value_band, key_pool, value_pool, key_coarse, value_coarse = carry
        group_index = block_index // N_SEQ
        seq_place = block_index % N_SEQ
        start = (block_index * BLOCK).astype(jnp.int32)
        group_start = (group_index * group_rows).astype(jnp.int32)
        query_block = lax.dynamic_slice_in_dim(query_rows, start, BLOCK)
        grad_block = lax.dynamic_slice_in_dim(grad_out, start, BLOCK)
        key_set = jnp.concatenate([lax.dynamic_slice_in_dim(padded_key, start, band), lax.dynamic_slice_in_dim(pooled_key, group_start, group_rows), coarse_key], axis=0)
        value_set = jnp.concatenate([lax.dynamic_slice_in_dim(padded_value, start, band), lax.dynamic_slice_in_dim(pooled_value, group_start, group_rows), coarse_value], axis=0)
        tokens = start + band_offsets
        live = jnp.concatenate([(tokens >= 0) & (tokens < total_tokens), jnp.abs(pool_block - seq_place) > 1, coarse_group != group_index])
        bias_row = jnp.where(live, 0.0, NEG_FILL).astype(jnp.float32)
        attended, grad_query, key_grads, value_grads = attend_block(query_block, grad_block, key_set, value_set, bias_row)
        key_band = add_rows(key_band, key_grads[:band], start)
        value_band = add_rows(value_band, value_grads[:band], start)
        key_pool = add_rows(key_pool, key_grads[band:band + group_rows], group_start)
        value_pool = add_rows(value_pool, value_grads[band:band + group_rows], group_start)
        key_coarse = key_coarse + key_grads[band + group_rows:]
        value_coarse = value_coarse + value_grads[band + group_rows:]
        return (key_band, value_band, key_pool, value_pool, key_coarse, value_coarse), (attended, grad_query)

    initial = (jnp.zeros((total_tokens + 2 * NEAR, WIDTH), jnp.float32), jnp.zeros((total_tokens + 2 * NEAR, WIDTH), jnp.float32), jnp.zeros((blocks * rows_one, WIDTH), jnp.float32), jnp.zeros((blocks * rows_one, WIDTH), jnp.float32), jnp.zeros((blocks * rows_two, WIDTH), jnp.float32), jnp.zeros((blocks * rows_two, WIDTH), jnp.float32))
    carry, outputs = lax.scan(visit, initial, jnp.arange(blocks, dtype=jnp.int32))
    key_band, value_band, key_pool, value_pool, key_coarse, value_coarse = carry
    attended = outputs[0].reshape(total_tokens, WIDTH)
    grad_query = outputs[1].reshape(total_tokens, WIDTH)
    key_pool_total = key_pool + expand_rows(key_coarse, MERGE) / MERGE
    value_pool_total = value_pool + expand_rows(value_coarse, MERGE) / MERGE
    grad_key = (key_band[NEAR:NEAR + total_tokens] + expand_rows(key_pool_total, POOL1) / POOL1).astype(jnp.bfloat16)
    grad_value = (value_band[NEAR:NEAR + total_tokens] + expand_rows(value_pool_total, POOL1) / POOL1).astype(jnp.bfloat16)
    return (attended, grad_query, grad_key, grad_value)
```

```python
import functools

import jax
import jax.numpy as jnp
from jax import lax
from jax.experimental import pallas as pl
from jax.experimental.pallas import tpu as pltpu
from jax.sharding import PartitionSpec as P

F32 = jnp.float32
BF16 = jnp.bfloat16
HEADS = 8
DIM = 128
BLOCK = 512
NEAR = 256
POOL = 16
ONE = BLOCK // POOL
TWO = ONE // POOL
PLACES = 16
GROUPS = 16
SET = 2048
OWN, PREV, NEXT, LEVEL1, LEVEL2 = 0, 512, 768, 1024, 1536
SCALE = DIM**-0.5
SCALE2 = SCALE * 1.4426950408889634
FILL = -1e30
MESH = pl.DeviceIdType.MESH
CHUNKS = 4
PER = HEADS // CHUNKS
STEP = 512

IN_KV, IN_QG, POOLED, FROM_PREV, FROM_NEXT, COARSE, PAIR_ONE, PAIR_TWO = range(8)
GRAD_PREV, GRAD_NEXT, PAIR_GRAD, COARSE_GRAD, POOL_GRAD, OUT_Q, OUT_KV = range(8, 15)
STAGES = 15


def dot_nt(a, b):
    return lax.dot_general(a, b, (((1,), (1,)), ((), ())), preferred_element_type=F32)


def dot_tn(a, b):
    return lax.dot_general(a, b, (((0,), (0,)), ((), ())), preferred_element_type=F32)


def dot_nn(a, b):
    return jnp.dot(a, b, preferred_element_type=F32)


def attend(h, q_all, g_all, kv, bias, att, gq, gown, gset, score, dprob, total):
    query, grad = q_all[h], g_all[h]
    parts = [pl.ds(i * STEP, STEP) for i in range(SET // STEP)]

    def folded(x, op):
        return op(x.reshape(STEP // 8, 8, BLOCK), axis=0)

    top = None
    for rows in parts:
        s = dot_nt(kv[h, 0, rows, :], query)
        b = bias[rows, :]
        s = s + jnp.concatenate([b] * (BLOCK // DIM), axis=1)
        score[rows, :] = s
        part = folded(s, jnp.max)
        top = part if top is None else jnp.maximum(top, part)
    top = jnp.max(top, axis=0, keepdims=True)
    norm = mixed = None
    for rows in parts:
        dp = dot_nt(kv[h, 1, rows, :], grad)
        e = jnp.exp2((score[rows, :] - top) * SCALE2)
        score[rows, :] = e
        dprob[rows, :] = dp
        part, other = folded(e, jnp.sum), folded(e * dp, jnp.sum)
        norm = part if norm is None else norm + part
        mixed = other if mixed is None else mixed + other
    inverse = 1.0 / jnp.sum(norm, axis=0, keepdims=True)
    delta = jnp.sum(mixed, axis=0, keepdims=True) * inverse
    for i, rows in enumerate(parts):
        p = score[rows, :] * inverse
        pb = p.astype(BF16)
        ds = (p * (dprob[rows, :] - delta)).astype(BF16)
        out, dq = dot_tn(kv[h, 1, rows, :], pb), dot_tn(kv[h, 0, rows, :], ds)
        if i == 0:
            total[0], total[1] = out, dq
        else:
            total[0] += out
            total[1] += dq
        dv, dk = dot_nn(pb, grad), dot_nn(ds, query) * SCALE
        if i * STEP < BLOCK:
            gown[h, 0, rows, :] = dk
            gown[h, 1, rows, :] = dv
        else:
            there = pl.ds(i * STEP - BLOCK, STEP)
            gset[h, 0, there, :] = dk.astype(BF16)
            gset[h, 1, there, :] = dv.astype(BF16)
    att[h] = total[0].T.astype(BF16)
    gq[h] = (total[1].T * SCALE).astype(BF16)


def kernel(
    q_hbm, k_hbm, v_hbm, g_hbm, att_hbm, gq_hbm, gk_hbm, gv_hbm,
    kv, q_all, g_all, pooled, gown, gset, pair, csend, crecv, psend, precv, hrecv,
    bias, mean, spread, score, dprob, total, att, gq, final, send, recv,
):
    g, s = lax.axis_index("grp"), lax.axis_index("seq")
    core = lax.rem(s, 2)
    other = 1 - core
    sibling = (g, s + 1 - 2 * core)
    has_prev = (g + s) > 0
    has_next = (g + s) < GROUPS + PLACES - 2
    up_group = lax.rem(g + lax.div(s + 1, PLACES), GROUPS)
    after = (up_group, lax.rem(s + 1, PLACES))
    low_group = lax.rem(g + GROUPS - 1 + lax.div(s + PLACES - 1, PLACES), GROUPS)
    before = (low_group, lax.rem(s + PLACES - 1, PLACES))
    mine_one = pl.multiple_of(s * ONE, ONE)
    mine_two = pl.multiple_of(g * ONE, ONE)

    def heads(ch):
        return pl.ds(ch * PER, PER)

    def lanes(h):
        return pl.ds(pl.multiple_of(h * DIM, DIM), DIM)

    def push(stage, ch, src, dst, device):
        pltpu.make_async_remote_copy(
            src_ref=src, dst_ref=dst, send_sem=send.at[stage, ch], recv_sem=recv.at[stage, ch],
            device_id=device, device_id_type=MESH,
        ).start()

    def await_bytes(sems, stage, ch, ref):
        pltpu.make_async_copy(ref, ref, sems.at[stage, ch]).wait()

    def each_head(ch, do):
        lax.fori_loop(0, PER, lambda i, _: (do(ch * PER + i), 0)[1], 0)

    def each_peer(do):
        lax.fori_loop(1, PLACES, lambda j, _: (do(j), 0)[1], 0)

    def fetch(h, _):
        ch = lax.div(h, PER)
        for plane, src in enumerate((k_hbm, v_hbm)):
            pltpu.make_async_copy(
                src.at[:, lanes(h)], kv.at[h, plane, pl.ds(OWN, BLOCK), :], recv.at[IN_KV, ch]
            ).start()
        for dst, src in ((q_all, q_hbm), (g_all, g_hbm)):
            pltpu.make_async_copy(src.at[:, lanes(h)], dst.at[h], recv.at[IN_QG, ch]).start()
        return 0

    lax.fori_loop(0, HEADS, fetch, 0)

    barrier = pltpu.get_barrier_semaphore()

    def greet(j):
        for device in ((g, lax.rem(s + j, PLACES)), (lax.rem(g + j, GROUPS), s)):
            pl.semaphore_signal(barrier, inc=1, device_id=device, device_id_type=MESH)

    each_peer(greet)
    crosses_up = jnp.logical_and(s == PLACES - 1, has_next)
    crosses_down = jnp.logical_and(s == 0, has_prev)

    @pl.when(crosses_up)
    def _():
        pl.semaphore_signal(barrier, inc=1, device_id=after, device_id_type=MESH)

    @pl.when(crosses_down)
    def _():
        pl.semaphore_signal(barrier, inc=1, device_id=before, device_id_type=MESH)

    row = lax.broadcasted_iota(jnp.int32, (SET, DIM), 0)
    one = lax.shift_right_logical(row - LEVEL1, 5)
    two = lax.shift_right_logical(row - LEVEL2, 5)
    dead_one = (row >= LEVEL1) & (row < LEVEL2) & (one >= s - 1) & (one <= s + 1)
    dead_two = (row >= LEVEL2) & (two == g)
    no_prev = (row >= PREV) & (row < NEXT) & (g + s == 0)
    no_next = (row >= NEXT) & (row < LEVEL1) & (g + s == GROUPS + PLACES - 2)
    bias[...] = jnp.where(dead_one | dead_two | no_prev | no_next, FILL, 0.0)
    wide = (lax.broadcasted_iota(jnp.int32, (ONE, BLOCK), 0), lax.broadcasted_iota(jnp.int32, (ONE, BLOCK), 1))
    mean[...] = jnp.where(lax.shift_right_logical(wide[1], 4) == wide[0], 1.0 / POOL, 0.0).astype(BF16)
    tall = (lax.broadcasted_iota(jnp.int32, (BLOCK, ONE), 0), lax.broadcasted_iota(jnp.int32, (BLOCK, ONE), 1))
    spread[...] = jnp.where(lax.shift_right_logical(tall[0], 4) == tall[1], 1.0 / POOL, 0.0).astype(BF16)

    @pl.when(jnp.logical_not(has_prev))
    def _():
        kv[:, :, PREV:NEXT, :] = jnp.zeros((HEADS, 2, NEAR, DIM), BF16)
        hrecv[:, 0] = jnp.zeros((HEADS, 2, NEAR, DIM), BF16)

    @pl.when(jnp.logical_not(has_next))
    def _():
        kv[:, :, NEXT:LEVEL1, :] = jnp.zeros((HEADS, 2, NEAR, DIM), BF16)
        hrecv[:, 1] = jnp.zeros((HEADS, 2, NEAR, DIM), BF16)

    crosses = jnp.logical_or(crosses_up, crosses_down)

    @pl.when(crosses)
    def _():
        pl.semaphore_wait(barrier, PLACES + GROUPS - 1)

    @pl.when(jnp.logical_not(crosses))
    def _():
        pl.semaphore_wait(barrier, PLACES + GROUPS - 2)

    def spread_rows(x):
        high = x.astype(BF16)
        low = (x - high.astype(F32)).astype(BF16)
        return dot_nn(spread[...], high) + dot_nn(spread[...], low)

    def send_pooled(ch):
        hs = heads(ch)
        await_bytes(recv, IN_KV, ch, kv.at[hs, :, pl.ds(OWN, BLOCK), :])

        def pool(h):
            for plane in range(2):
                pooled[h, plane] = dot_nn(mean[...], kv[h, plane, pl.ds(OWN, BLOCK), :]).astype(BF16)
            kv[h, core, pl.ds(LEVEL1 + mine_one, ONE), :] = pooled[h, core]

        each_head(ch, pool)

        def to(j):
            there = lax.rem(s + j, PLACES)
            plane = lax.rem(there, 2)
            push(
                POOLED, ch, pooled.at[hs, plane],
                kv.at[hs, plane, pl.ds(LEVEL1 + mine_one, ONE), :], (g, there),
            )

        each_peer(to)

        @pl.when(has_next)
        def _():
            push(FROM_PREV, ch, kv.at[hs, :, pl.ds(OWN + BLOCK - NEAR, NEAR), :], kv.at[hs, :, pl.ds(PREV, NEAR), :], after)

        @pl.when(has_prev)
        def _():
            push(FROM_NEXT, ch, kv.at[hs, :, pl.ds(OWN, NEAR), :], kv.at[hs, :, pl.ds(NEXT, NEAR), :], before)

    def all_but_one(ref, ch):
        return ref.at[heads(ch), pl.ds(0, BLOCK - ONE), :]

    def send_coarse(ch):
        hs = heads(ch)
        await_bytes(recv, POOLED, ch, kv.at[hs, core, pl.ds(LEVEL1, BLOCK - ONE), :])
        whole = kv.at[hs, core, pl.ds(LEVEL1, BLOCK), :]
        push(PAIR_ONE, ch, whole, whole, sibling)

        def pool(h):
            kv[h, core, pl.ds(LEVEL2 + mine_two, ONE), :] = dot_nn(
                mean[...], kv[h, core, pl.ds(LEVEL1, BLOCK), :]
            ).astype(BF16)

        each_head(ch, pool)
        own = kv.at[hs, core, pl.ds(LEVEL2 + mine_two, ONE), :]
        each_peer(lambda j: push(COARSE, ch, own, own, (lax.rem(g + j, GROUPS), s)))

    def pass_coarse(ch):
        hs = heads(ch)
        await_bytes(recv, COARSE, ch, kv.at[hs, core, pl.ds(LEVEL2, BLOCK - ONE), :])
        whole = kv.at[hs, core, pl.ds(LEVEL2, BLOCK), :]
        push(PAIR_TWO, ch, whole, whole, sibling)

    def compute(ch):
        hs = heads(ch)
        await_bytes(recv, IN_QG, ch, kv.at[hs, :, pl.ds(OWN, BLOCK), :])
        await_bytes(recv, PAIR_ONE, ch, kv.at[hs, other, pl.ds(LEVEL1, BLOCK), :])
        await_bytes(recv, PAIR_TWO, ch, kv.at[hs, other, pl.ds(LEVEL2, BLOCK), :])

        @pl.when(has_prev)
        def _():
            await_bytes(recv, FROM_PREV, ch, kv.at[hs, :, pl.ds(PREV, NEAR), :])

        @pl.when(has_next)
        def _():
            await_bytes(recv, FROM_NEXT, ch, kv.at[hs, :, pl.ds(NEXT, NEAR), :])

        each_head(
            ch,
            lambda h: attend(h, q_all, g_all, kv, bias, att, gq, gown, gset, score, dprob, total),
        )
        push(PAIR_GRAD, ch, gset.at[hs, other, pl.ds(LEVEL1 - BLOCK, 2 * BLOCK), :], pair.at[hs], sibling)

        @pl.when(has_prev)
        def _():
            push(GRAD_NEXT, ch, gset.at[hs, :, pl.ds(PREV - BLOCK, NEAR), :], hrecv.at[hs, 1], before)

        @pl.when(has_next)
        def _():
            push(GRAD_PREV, ch, gset.at[hs, :, pl.ds(NEXT - BLOCK, NEAR), :], hrecv.at[hs, 0], after)

        def store(h):
            for src, dst in ((att, att_hbm), (gq, gq_hbm)):
                pltpu.make_async_copy(src.at[h], dst.at[:, lanes(h)], send.at[OUT_Q, ch]).start()

        each_head(ch, store)

    def send_coarse_grads(ch):
        hs = heads(ch)
        await_bytes(recv, PAIR_GRAD, ch, pair.at[hs])

        def add(h):
            mine = gset[h, core, pl.ds(LEVEL2 - BLOCK, BLOCK), :].astype(F32)
            csend[h] = (mine + pair[h, pl.ds(BLOCK, BLOCK), :].astype(F32)).astype(BF16)
            crecv[h, pl.ds(mine_two, ONE), :] = csend[h, pl.ds(mine_two, ONE), :]

        each_head(ch, add)

        def to(j):
            there = lax.rem(g + j, GROUPS)
            rows = pl.ds(pl.multiple_of(there * ONE, ONE), ONE)
            push(COARSE_GRAD, ch, csend.at[hs, rows, :], crecv.at[hs, pl.ds(mine_two, ONE), :], (there, s))

        each_peer(to)

    def send_pool_grads(ch):
        hs = heads(ch)
        await_bytes(recv, COARSE_GRAD, ch, all_but_one(crecv, ch))

        def add(h):
            coarse = crecv[h, pl.ds(0, ONE), :].astype(F32)
            for i in range(1, GROUPS):
                coarse = coarse + crecv[h, pl.ds(i * ONE, ONE), :].astype(F32)
            mine = gset[h, core, pl.ds(LEVEL1 - BLOCK, BLOCK), :].astype(F32)
            both = mine + pair[h, pl.ds(0, BLOCK), :].astype(F32)
            psend[h] = (both + spread_rows(coarse)).astype(BF16)
            precv[h, pl.ds(mine_one, ONE), :] = psend[h, pl.ds(mine_one, ONE), :]

        each_head(ch, add)

        def to(j):
            there = lax.rem(s + j, PLACES)
            rows = pl.ds(pl.multiple_of(there * ONE, ONE), ONE)
            push(POOL_GRAD, ch, psend.at[hs, rows, :], precv.at[hs, pl.ds(mine_one, ONE), :], (g, there))

        each_peer(to)

    def finish(ch):
        hs = heads(ch)
        await_bytes(recv, POOL_GRAD, ch, all_but_one(precv, ch))

        @pl.when(has_prev)
        def _():
            await_bytes(recv, GRAD_PREV, ch, hrecv.at[hs, 0])

        @pl.when(has_next)
        def _():
            await_bytes(recv, GRAD_NEXT, ch, hrecv.at[hs, 1])

        def add(h):
            for plane, dst in enumerate((gk_hbm, gv_hbm)):
                level = precv[h, pl.ds(plane * ONE, ONE), :].astype(F32)
                for i in range(1, PLACES // 2):
                    level = level + precv[h, pl.ds((2 * i + plane) * ONE, ONE), :].astype(F32)
                sums = gown[h, plane] + spread_rows(level)
                for side in range(2):
                    rows = slice(side * NEAR, (side + 1) * NEAR)
                    final[h, plane, pl.ds(side * NEAR, NEAR), :] = (
                        sums[rows] + hrecv[h, side, plane].astype(F32)
                    ).astype(BF16)
                pltpu.make_async_copy(final.at[h, plane], dst.at[:, lanes(h)], send.at[OUT_KV, ch]).start()

        each_head(ch, add)

    stages = (send_pooled, send_coarse, pass_coarse, compute, send_coarse_grads, send_pool_grads, finish)

    def step(t, _):
        for lag, stage in enumerate(stages):
            pl.when(jnp.logical_and(t >= lag, t < CHUNKS + lag))(functools.partial(stage, t - lag))
        return 0

    lax.fori_loop(0, CHUNKS + len(stages) - 1, step, 0)

    def drain(ch, _):
        hs = heads(ch)
        for stage, ref in (
            (POOLED, all_but_one(psend, ch)),
            (COARSE, all_but_one(psend, ch)),
            (PAIR_ONE, psend.at[hs]),
            (PAIR_TWO, psend.at[hs]),
            (PAIR_GRAD, pair.at[hs]),
            (COARSE_GRAD, all_but_one(csend, ch)),
            (POOL_GRAD, all_but_one(psend, ch)),
            (OUT_Q, pair.at[hs]),
            (OUT_KV, final.at[hs]),
        ):
            await_bytes(send, stage, ch, ref)

        @pl.when(has_prev)
        def _():
            await_bytes(send, FROM_NEXT, ch, hrecv.at[hs, 0])
            await_bytes(send, GRAD_NEXT, ch, hrecv.at[hs, 0])

        @pl.when(has_next)
        def _():
            await_bytes(send, FROM_PREV, ch, hrecv.at[hs, 0])
            await_bytes(send, GRAD_PREV, ch, hrecv.at[hs, 0])

        return 0

    lax.fori_loop(0, CHUNKS, drain, 0)


def body(query_rows, key_rows, value_rows, grad_out):
    shape = jax.ShapeDtypeStruct(query_rows.shape, BF16)
    rows = (HEADS, BLOCK, DIM)
    scratch = [
        ((HEADS, 2, SET, DIM), BF16),
        (rows, BF16),
        (rows, BF16),
        ((HEADS, 2, ONE, DIM), BF16),
        ((HEADS, 2, BLOCK, DIM), F32),
        ((HEADS, 2, SET - BLOCK, DIM), BF16),
        ((HEADS, 2 * BLOCK, DIM), BF16),
        (rows, BF16),
        (rows, BF16),
        (rows, BF16),
        (rows, BF16),
        ((HEADS, 2, 2, NEAR, DIM), BF16),
        ((SET, DIM), F32),
        ((ONE, BLOCK), BF16),
        ((BLOCK, ONE), BF16),
        ((SET, BLOCK), F32),
        ((SET, BLOCK), F32),
        ((2, DIM, BLOCK), F32),
        (rows, BF16),
        (rows, BF16),
        ((HEADS, 2, BLOCK, DIM), BF16),
    ]
    anywhere = pl.BlockSpec(memory_space=pl.ANY)
    return pl.pallas_call(
        kernel,
        out_shape=[shape] * 4,
        in_specs=[anywhere] * 4,
        out_specs=[anywhere] * 4,
        scratch_shapes=[pltpu.VMEM(*one) for one in scratch]
        + [pltpu.SemaphoreType.DMA((STAGES, CHUNKS))] * 2,
        compiler_params=pltpu.CompilerParams(
            collective_id=0, has_side_effects=True, vmem_limit_bytes=58 << 20
        ),
        name="hierarchical",
    )(query_rows, key_rows, value_rows, grad_out)


def solution(mesh):
    placed = P(("grp", "seq"), None)
    return jax.shard_map(
        body, mesh=mesh, in_specs=(placed,) * 4, out_specs=(placed,) * 4, check_vma=False
    )
```

```python
import functools

import jax
import jax.numpy as jnp
from jax import lax
from jax.experimental import pallas as pl
from jax.experimental.pallas import tpu as pltpu
from jax.sharding import PartitionSpec as P

F32 = jnp.float32
BF16 = jnp.bfloat16
HEADS = 8
DIM = 128
BLOCK = 512
NEAR = 256
POOL = 16
ONE = BLOCK // POOL
TWO = ONE // POOL
PLACES = 16
GROUPS = 16
SET = 2048
OWN, PREV, NEXT, LEVEL1, LEVEL2 = 0, 512, 768, 1024, 1536
SCALE = DIM**-0.5
SCALE2 = SCALE * 1.4426950408889634
FILL = -1e30
MESH = pl.DeviceIdType.MESH
CHUNKS = 8
PER = HEADS // CHUNKS
STEP = 512

IN_KV, IN_QG, PAIR_POOL, ACROSS_HI, RIGHT, LEFT = range(0, 6)
FAR_RIGHT, FAR_LEFT, ACROSS_LO, UP1, DOWN1, UP2 = range(6, 12)
DOWN2, UP3, DOWN3, UP4, DOWN4, PAIR_SET = range(12, 18)
FROM_PREV, FROM_NEXT, PAIR_GRAD, GRAD_PREV, GRAD_NEXT, C_DOWN3 = range(18, 24)
C_UP3, C_DOWN4, C_UP4, C_DOWN1, C_UP1, C_DOWN2 = range(24, 30)
C_UP2, C_LO, R_FAR_LEFT, R_FAR_RIGHT, R_LEFT, R_RIGHT = range(30, 36)
R_HI, R_PAIR = range(36, 38)
TRANSFERS = 38


def dot_nt(a, b):
    return lax.dot_general(a, b, (((1,), (1,)), ((), ())), preferred_element_type=F32)


def dot_tn(a, b):
    return lax.dot_general(a, b, (((0,), (0,)), ((), ())), preferred_element_type=F32)


def dot_nn(a, b):
    return jnp.dot(a, b, preferred_element_type=F32)


def attend(h, q_all, g_all, kv, bias, att, gq, gown, gset, score, dprob, total):
    query, grad = q_all[h], g_all[h]
    parts = [pl.ds(i * STEP, STEP) for i in range(SET // STEP)]

    def folded(x, op):
        return op(x.reshape(STEP // 8, 8, BLOCK), axis=0)

    top = None
    for rows in parts:
        s = dot_nt(kv[h, 0, rows, :], query)
        b = bias[rows, :]
        s = s + jnp.concatenate([b] * (BLOCK // DIM), axis=1)
        score[rows, :] = s
        part = folded(s, jnp.max)
        top = part if top is None else jnp.maximum(top, part)
    top = jnp.max(top, axis=0, keepdims=True)
    norm = mixed = None
    for rows in parts:
        dp = dot_nt(kv[h, 1, rows, :], grad)
        e = jnp.exp2((score[rows, :] - top) * SCALE2)
        score[rows, :] = e
        dprob[rows, :] = dp
        part, other = folded(e, jnp.sum), folded(e * dp, jnp.sum)
        norm = part if norm is None else norm + part
        mixed = other if mixed is None else mixed + other
    inverse = 1.0 / jnp.sum(norm, axis=0, keepdims=True)
    delta = jnp.sum(mixed, axis=0, keepdims=True) * inverse
    for i, rows in enumerate(parts):
        p = score[rows, :] * inverse
        pb = p.astype(BF16)
        ds = (p * (dprob[rows, :] - delta)).astype(BF16)
        out, dq = dot_tn(kv[h, 1, rows, :], pb), dot_tn(kv[h, 0, rows, :], ds)
        if i == 0:
            total[0], total[1] = out, dq
        else:
            total[0] += out
            total[1] += dq
        dv, dk = dot_nn(pb, grad), dot_nn(ds, query) * SCALE
        if i * STEP < BLOCK:
            gown[h, 0, rows, :] = dk
            gown[h, 1, rows, :] = dv
        else:
            there = pl.ds(i * STEP - BLOCK, STEP)
            gset[h, 0, there, :] = dk.astype(BF16)
            gset[h, 1, there, :] = dv.astype(BF16)
    lanes = pl.ds(pl.multiple_of(h * DIM, DIM), DIM)
    att[:, lanes] = total[0].T.astype(BF16)
    gq[:, lanes] = (total[1].T * SCALE).astype(BF16)


def kernel(
    q_hbm, k_hbm, v_hbm, g_hbm, att, gq, gk, gv,
    kv, q_all, g_all, pooled, told, heard, gown, gset, pair, csend, cfar, cnear, clow,
    psend, rfar, rnear, rlow, level, lsend, hrecv, bias, mean, spread, score, dprob, total,
    send, recv, told_sem, heard_sem,
):
    g, s = lax.axis_index("grp"), lax.axis_index("seq")
    low, z = lax.div(g, 8), lax.rem(g, 8)
    high, x, core = lax.div(s, 8), lax.div(lax.rem(s, 8), 2), lax.rem(s, 2)
    other = 1 - core
    sibling = (g, s + 1 - 2 * core)
    across_hi = (g, (1 - high) * 8 + x * 2 + core)
    across_lo = ((1 - low) * 8 + z, s)
    slot_one = x * 4 + high * 2 + core
    slot_two = z * 2 + low
    has_prev = (g + s) > 0
    has_next = (g + s) < GROUPS + PLACES - 2
    up_group = lax.rem(g + lax.div(s + 1, PLACES), GROUPS)
    after = (up_group, lax.rem(s + 1, PLACES))
    low_group = lax.rem(g + GROUPS - 1 + lax.div(s + PLACES - 1, PLACES), GROUPS)
    before = (low_group, lax.rem(s + PLACES - 1, PLACES))

    def near_x(d):
        return lax.rem(x + d + 4, 4)

    def near_z(d):
        return lax.rem(z + d + 8, 8)

    def beside(d):
        return (g, high * 8 + near_x(d) * 2 + core)

    def along(d):
        return (low * 8 + near_z(d), s)

    def ranks(start, unit, count):
        return pl.ds(pl.multiple_of(start * unit, unit), count)

    def one_rows(column, row, count):
        return ranks(LEVEL1 // ONE + column * 4 + row * 2, ONE, count)

    def two_rows(column, row, count):
        return ranks(LEVEL2 // ONE + column * 2 + row, ONE, count)

    def heads(ch):
        return pl.ds(ch * PER, PER)

    def lanes(h):
        return pl.ds(pl.multiple_of(h * DIM, DIM), DIM)

    def push(transfer, ch, src, dst, device):
        pltpu.make_async_remote_copy(
            src_ref=src, dst_ref=dst, send_sem=send.at[transfer, ch], recv_sem=recv.at[transfer, ch],
            device_id=device, device_id_type=MESH,
        ).start()

    def await_rows(sems, transfer, ch, rows):
        ref = kv.at[heads(ch), 0, pl.ds(0, rows), :]
        pltpu.make_async_copy(ref, ref, sems.at[transfer, ch]).wait()

    def each_head(ch, do):
        lax.fori_loop(0, PER, lambda i, _: (do(ch * PER + i), 0)[1], 0)

    def each_peer(do):
        lax.fori_loop(1, PLACES, lambda j, _: (do(j), 0)[1], 0)

    def fetch(h, _):
        ch = lax.div(h, PER)
        for plane, src in enumerate((k_hbm, v_hbm)):
            pltpu.make_async_copy(
                src.at[:, lanes(h)], kv.at[h, plane, pl.ds(OWN, BLOCK), :], recv.at[IN_KV, ch]
            ).start()
        return 0

    def fetch_more(h, _):
        ch = lax.div(h, PER)
        for dst, src in ((q_all, q_hbm), (g_all, g_hbm)):
            pltpu.make_async_copy(src.at[:, lanes(h)], dst.at[h], recv.at[IN_QG, ch]).start()
        return 0

    lax.fori_loop(0, HEADS, fetch, 0)
    lax.fori_loop(0, HEADS, fetch_more, 0)

    barrier = pltpu.get_barrier_semaphore()

    def greet(j):
        for device in ((g, lax.rem(s + j, PLACES)), (lax.rem(g + j, GROUPS), s)):
            pl.semaphore_signal(barrier, inc=1, device_id=device, device_id_type=MESH)

    each_peer(greet)
    crosses_up = jnp.logical_and(s == PLACES - 1, has_next)
    crosses_down = jnp.logical_and(s == 0, has_prev)

    @pl.when(crosses_up)
    def _():
        pl.semaphore_signal(barrier, inc=1, device_id=after, device_id_type=MESH)

    @pl.when(crosses_down)
    def _():
        pl.semaphore_signal(barrier, inc=1, device_id=before, device_id_type=MESH)

    wide = (lax.broadcasted_iota(jnp.int32, (ONE, BLOCK), 0), lax.broadcasted_iota(jnp.int32, (ONE, BLOCK), 1))
    mean[...] = jnp.where(lax.shift_right_logical(wide[1], 4) == wide[0], 1.0 / POOL, 0.0).astype(BF16)
    tall = (lax.broadcasted_iota(jnp.int32, (BLOCK, ONE), 0), lax.broadcasted_iota(jnp.int32, (BLOCK, ONE), 1))
    spread[...] = jnp.where(lax.shift_right_logical(tall[0], 4) == tall[1], 1.0 / POOL, 0.0).astype(BF16)

    def pool_own(h, _):
        @pl.when(lax.rem(h, PER) == 0)
        def _():
            await_rows(recv, IN_KV, lax.div(h, PER), 2 * BLOCK)

        for plane in range(2):
            pooled[plane, h] = dot_nn(mean[...], kv[h, plane, pl.ds(OWN, BLOCK), :]).astype(BF16)
        kv[h, core, ranks(LEVEL1 // ONE + slot_one, ONE, ONE), :] = pooled[core, h]
        return 0

    lax.fori_loop(0, HEADS, pool_own, 0)
    told[...] = dot_nn(mean[...], pooled[...].reshape(2 * HEADS * ONE, DIM)).astype(BF16)
    heard[slot_one] = told[...]

    @pl.when(jnp.logical_not(has_prev))
    def _():
        kv[:, :, PREV:NEXT, :] = jnp.zeros((HEADS, 2, NEAR, DIM), BF16)
        hrecv[:, 0] = jnp.zeros((HEADS, 2, NEAR, DIM), BF16)

    @pl.when(jnp.logical_not(has_next))
    def _():
        kv[:, :, NEXT:LEVEL1, :] = jnp.zeros((HEADS, 2, NEAR, DIM), BF16)
        hrecv[:, 1] = jnp.zeros((HEADS, 2, NEAR, DIM), BF16)

    crosses = jnp.logical_or(crosses_up, crosses_down)

    @pl.when(crosses)
    def _():
        pl.semaphore_wait(barrier, PLACES + GROUPS - 1)

    @pl.when(jnp.logical_not(crosses))
    def _():
        pl.semaphore_wait(barrier, PLACES + GROUPS - 2)

    def tell(j):
        pltpu.make_async_remote_copy(
            src_ref=told, dst_ref=heard.at[slot_one], send_sem=told_sem.at[0], recv_sem=heard_sem.at[0],
            device_id=(g, lax.rem(s + j, PLACES)), device_id_type=MESH,
        ).start()

    each_peer(tell)

    def spread_rows(v):
        upper = v.astype(BF16)
        rest = (v - upper.astype(F32)).astype(BF16)
        return dot_nn(spread[...], upper) + dot_nn(spread[...], rest)

    def swap_pooled(ch):
        hs = heads(ch)
        push(PAIR_POOL, ch, pooled.at[other, hs], kv.at[hs, other, ranks(LEVEL1 // ONE + slot_one, ONE, ONE), :], sibling)

    def tables():
        row = lax.broadcasted_iota(jnp.int32, (SET, DIM), 0)
        slot = lax.shift_right_logical(row & (BLOCK - 1), 5)
        place = (lax.shift_right_logical(slot, 1) & 1) * 8 + lax.shift_right_logical(slot, 2) * 2 + (slot & 1)
        group = (slot & 1) * 8 + lax.shift_right_logical(slot, 1)
        dead_one = (row >= LEVEL1) & (row < LEVEL2) & (place >= s - 1) & (place <= s + 1)
        dead_two = (row >= LEVEL2) & (group == g)
        no_prev = (row >= PREV) & (row < NEXT) & (g + s == 0)
        no_next = (row >= NEXT) & (row < LEVEL1) & (g + s == GROUPS + PLACES - 2)
        bias[...] = jnp.where(dead_one | dead_two | no_prev | no_next, FILL, 0.0)

    def own_coarse():
        pltpu.make_async_copy(heard.at[pl.ds(0, PLACES - 1)], heard.at[pl.ds(0, PLACES - 1)], heard_sem.at[0]).wait()
        shape = (HEADS * ONE, PLACES * ONE)
        to, come = lax.broadcasted_iota(jnp.int32, shape, 0), lax.broadcasted_iota(jnp.int32, shape, 1)
        head, within = lax.shift_right_logical(to, 5), to & 31
        wanted = lax.shift_right_logical(within, 1) * ONE + core * 16 + head * 2 + (within & 1)
        pick = jnp.where(come == wanted, 1.0, 0.0).astype(BF16)
        rows = dot_nn(pick, heard[...].reshape(PLACES * ONE, DIM)).astype(BF16)
        for h in range(HEADS):
            kv[h, core, ranks(LEVEL2 // ONE + slot_two, ONE, ONE), :] = rows[h * ONE : (h + 1) * ONE]

    def swap_across(ch):
        hs = heads(ch)
        await_rows(recv, PAIR_POOL, ch, ONE)
        chip = kv.at[hs, core, one_rows(x, high, 2 * ONE), :]
        push(ACROSS_HI, ch, chip, chip, across_hi)

        @pl.when(ch == 0)
        def _():
            tables()
            own_coarse()

        group = kv.at[hs, core, two_rows(z, low, ONE), :]
        push(ACROSS_LO, ch, group, group, across_lo)

    def send_beside(ch):
        hs = heads(ch)
        await_rows(recv, ACROSS_HI, ch, 2 * ONE)
        column = kv.at[hs, core, one_rows(x, 0, 4 * ONE), :]
        push(RIGHT, ch, column, column, beside(1))
        push(LEFT, ch, column, column, beside(-1))
        await_rows(recv, ACROSS_LO, ch, ONE)
        both = kv.at[hs, core, two_rows(z, 0, 2 * ONE), :]
        for transfer, d in ((UP2, 2), (DOWN2, -2), (UP1, 1), (DOWN1, -1)):
            push(transfer, ch, both, both, along(d))

    def send_on(ch):
        hs = heads(ch)
        await_rows(recv, RIGHT, ch, 4 * ONE)
        part = kv.at[hs, core, one_rows(near_x(-1), 0, 2 * ONE), :]
        push(FAR_RIGHT, ch, part, part, beside(1))
        await_rows(recv, LEFT, ch, 4 * ONE)
        part = kv.at[hs, core, one_rows(near_x(1), 1, 2 * ONE), :]
        push(FAR_LEFT, ch, part, part, beside(-1))
        await_rows(recv, UP2, ch, 2 * ONE)
        both = kv.at[hs, core, two_rows(near_z(-2), 0, 2 * ONE), :]
        push(UP3, ch, both, both, along(1))
        part = kv.at[hs, core, two_rows(near_z(-2), 0, ONE), :]
        push(UP4, ch, part, part, along(2))
        await_rows(recv, DOWN2, ch, 2 * ONE)
        both = kv.at[hs, core, two_rows(near_z(2), 0, 2 * ONE), :]
        push(DOWN3, ch, both, both, along(-1))
        part = kv.at[hs, core, two_rows(near_z(2), 1, ONE), :]
        push(DOWN4, ch, part, part, along(-2))

        @pl.when(has_next)
        def _():
            push(FROM_PREV, ch, kv.at[hs, :, pl.ds(OWN + BLOCK - NEAR, NEAR), :], kv.at[hs, :, pl.ds(PREV, NEAR), :], after)

        @pl.when(has_prev)
        def _():
            push(FROM_NEXT, ch, kv.at[hs, :, pl.ds(OWN, NEAR), :], kv.at[hs, :, pl.ds(NEXT, NEAR), :], before)

    def swap_set(ch):
        hs = heads(ch)
        for transfer, rows in (
            (FAR_RIGHT, 2), (FAR_LEFT, 2), (UP1, 2), (DOWN1, 2), (UP3, 2), (DOWN3, 2), (UP4, 1), (DOWN4, 1),
        ):
            await_rows(recv, transfer, ch, rows * ONE)
        whole = kv.at[hs, core, pl.ds(LEVEL1, 2 * BLOCK), :]
        push(PAIR_SET, ch, whole, whole, sibling)

    def compute(ch):
        hs = heads(ch)
        await_rows(recv, IN_QG, ch, 2 * BLOCK)
        await_rows(recv, PAIR_SET, ch, 2 * BLOCK)

        @pl.when(has_prev)
        def _():
            await_rows(recv, FROM_PREV, ch, 2 * NEAR)

        @pl.when(has_next)
        def _():
            await_rows(recv, FROM_NEXT, ch, 2 * NEAR)

        each_head(
            ch,
            lambda h: attend(h, q_all, g_all, kv, bias, att, gq, gown, gset, score, dprob, total),
        )
        push(PAIR_GRAD, ch, gset.at[hs, other, pl.ds(LEVEL1 - BLOCK, 2 * BLOCK), :], pair.at[hs], sibling)

        @pl.when(has_prev)
        def _():
            push(GRAD_NEXT, ch, gset.at[hs, :, pl.ds(PREV - BLOCK, NEAR), :], hrecv.at[hs, 1], before)

        @pl.when(has_next)
        def _():
            push(GRAD_PREV, ch, gset.at[hs, :, pl.ds(NEXT - BLOCK, NEAR), :], hrecv.at[hs, 0], after)

    def added(a, b):
        return (a.astype(F32) + b.astype(F32)).astype(BF16)

    def group_rows(d, row, count):
        return ranks(near_z(d) * 2 + row, ONE, count)

    def place_rows(d, row, count):
        return ranks(near_x(d) * 4 + row * 2, ONE, count)

    def coarse_far(ch):
        hs = heads(ch)
        await_rows(recv, PAIR_GRAD, ch, 2 * BLOCK)

        def add(h):
            csend[h] = added(gset[h, core, pl.ds(LEVEL2 - BLOCK, BLOCK), :], pair[h, pl.ds(BLOCK, BLOCK), :])

        each_head(ch, add)
        push(C_DOWN4, ch, csend.at[hs, group_rows(-4, 0, ONE), :], cfar.at[hs, pl.ds(128, ONE), :], along(-2))
        push(C_UP4, ch, csend.at[hs, group_rows(4, 1, ONE), :], cfar.at[hs, pl.ds(160, ONE), :], along(2))
        push(C_DOWN3, ch, csend.at[hs, group_rows(-3, 0, 2 * ONE), :], cfar.at[hs, pl.ds(0, 64), :], along(-1))
        push(C_UP3, ch, csend.at[hs, group_rows(3, 0, 2 * ONE), :], cfar.at[hs, pl.ds(64, 64), :], along(1))

    def coarse_near(ch):
        hs = heads(ch)
        await_rows(recv, C_DOWN3, ch, 2 * ONE)
        await_rows(recv, C_UP3, ch, 2 * ONE)
        await_rows(recv, C_DOWN4, ch, ONE)
        await_rows(recv, C_UP4, ch, ONE)

        def add(h):
            for d, at, row, more in ((-2, 0, 0, 128), (2, 64, 1, 160)):
                for k in range(2):
                    rows = group_rows(d, k, ONE)
                    v = csend[h, rows, :].astype(F32) + cfar[h, pl.ds(at + k * ONE, ONE), :].astype(F32)
                    if k == row:
                        v = v + cfar[h, pl.ds(more, ONE), :].astype(F32)
                    csend[h, rows, :] = v.astype(BF16)

        each_head(ch, add)
        for i, (transfer, d) in enumerate(((C_UP2, 2), (C_DOWN2, -2), (C_UP1, 1), (C_DOWN1, -1))):
            push(transfer, ch, csend.at[hs, group_rows(d, 0, 64), :], cnear.at[hs, pl.ds(i * 64, 64), :], along(d))

    def coarse_low(ch):
        hs = heads(ch)
        for transfer in (C_UP2, C_DOWN2, C_UP1, C_DOWN1):
            await_rows(recv, transfer, ch, 2 * ONE)

        def add(h):
            rows = group_rows(0, 0, 64)
            v = csend[h, rows, :].astype(F32)
            for i in range(4):
                v = v + cnear[h, pl.ds(i * 64, 64), :].astype(F32)
            csend[h, rows, :] = v.astype(BF16)

        each_head(ch, add)
        push(C_LO, ch, csend.at[hs, group_rows(0, 1 - low, ONE), :], clow.at[hs], across_lo)

    def pool_far(ch):
        hs = heads(ch)
        await_rows(recv, C_LO, ch, ONE)

        def add(h):
            coarse = csend[h, group_rows(0, low, ONE), :].astype(F32) + clow[h].astype(F32)
            mine = gset[h, core, pl.ds(LEVEL1 - BLOCK, BLOCK), :].astype(F32)
            both = mine + pair[h, pl.ds(0, BLOCK), :].astype(F32)
            psend[h] = (both + spread_rows(coarse)).astype(BF16)

        each_head(ch, add)
        push(R_FAR_LEFT, ch, psend.at[hs, place_rows(-2, 0, 64), :], rfar.at[hs, pl.ds(0, 64), :], beside(-1))
        push(R_FAR_RIGHT, ch, psend.at[hs, place_rows(2, 1, 64), :], rfar.at[hs, pl.ds(64, 64), :], beside(1))

    def pool_near(ch):
        hs = heads(ch)
        await_rows(recv, R_FAR_LEFT, ch, 64)
        await_rows(recv, R_FAR_RIGHT, ch, 64)

        def add(h):
            for d, row in ((-1, 0), (1, 1)):
                rows = place_rows(d, row, 64)
                psend[h, rows, :] = added(psend[h, rows, :], rfar[h, pl.ds(row * 64, 64), :])

        each_head(ch, add)
        push(R_LEFT, ch, psend.at[hs, place_rows(-1, 0, 128), :], rnear.at[hs, pl.ds(0, 128), :], beside(-1))
        push(R_RIGHT, ch, psend.at[hs, place_rows(1, 0, 128), :], rnear.at[hs, pl.ds(128, 128), :], beside(1))

    def pool_high(ch):
        hs = heads(ch)
        await_rows(recv, R_LEFT, ch, 128)
        await_rows(recv, R_RIGHT, ch, 128)

        def add(h):
            rows = place_rows(0, 0, 128)
            v = psend[h, rows, :].astype(F32) + rnear[h, pl.ds(0, 128), :].astype(F32)
            psend[h, rows, :] = (v + rnear[h, pl.ds(128, 128), :].astype(F32)).astype(BF16)

        each_head(ch, add)
        push(R_HI, ch, psend.at[hs, place_rows(0, 1 - high, 64), :], rlow.at[hs], across_hi)

    def pool_pair(ch):
        hs = heads(ch)
        await_rows(recv, R_HI, ch, 64)

        def add(h):
            def sums(which):
                v = psend[h, ranks(x * 4 + high * 2 + which, ONE, ONE), :].astype(F32)
                return v + rlow[h, ranks(which, ONE, ONE), :].astype(F32)

            level[core, h] = sums(core)
            lsend[h] = sums(other)

        each_head(ch, add)
        push(R_PAIR, ch, lsend.at[hs], level.at[core, hs], sibling)

    def finish(ch):
        await_rows(recv, R_PAIR, ch, 2 * ONE)

        @pl.when(has_prev)
        def _():
            await_rows(recv, GRAD_PREV, ch, 2 * NEAR)

        @pl.when(has_next)
        def _():
            await_rows(recv, GRAD_NEXT, ch, 2 * NEAR)

        def add(h):
            for plane, dst in enumerate((gk, gv)):
                sums = gown[h, plane] + spread_rows(level[plane, h])
                for side in range(2):
                    rows = slice(side * NEAR, (side + 1) * NEAR)
                    dst[pl.ds(side * NEAR, NEAR), lanes(h)] = (
                        sums[rows] + hrecv[h, side, plane].astype(F32)
                    ).astype(BF16)

        each_head(ch, add)

    stages = (
        swap_pooled, swap_across, send_beside, send_on, swap_set, compute,
        coarse_far, coarse_near, coarse_low, pool_far, pool_near, pool_high, pool_pair, finish,
    )

    def step(t, _):
        for lag, stage in enumerate(stages):
            pl.when(jnp.logical_and(t >= lag, t < CHUNKS + lag))(functools.partial(stage, t - lag))
        return 0

    lax.fori_loop(0, CHUNKS + len(stages) - 1, step, 0)

    pltpu.make_async_copy(heard.at[pl.ds(0, PLACES - 1)], heard.at[pl.ds(0, PLACES - 1)], told_sem.at[0]).wait()

    def drain(ch, _):
        for rows, transfers in (
            (32, (PAIR_POOL, ACROSS_LO, UP4, DOWN4, C_DOWN4, C_UP4, C_LO)),
            (64, (ACROSS_HI, FAR_RIGHT, FAR_LEFT, UP1, DOWN1, UP2, DOWN2, UP3, DOWN3)),
            (64, (C_DOWN3, C_UP3, C_DOWN1, C_UP1, C_DOWN2, C_UP2, R_FAR_LEFT, R_FAR_RIGHT, R_HI, R_PAIR)),
            (128, (RIGHT, LEFT, R_LEFT, R_RIGHT)),
            (1024, (PAIR_SET, PAIR_GRAD)),
        ):
            for transfer in transfers:
                await_rows(send, transfer, ch, rows)

        @pl.when(has_prev)
        def _():
            await_rows(send, FROM_NEXT, ch, 2 * NEAR)
            await_rows(send, GRAD_NEXT, ch, 2 * NEAR)

        @pl.when(has_next)
        def _():
            await_rows(send, FROM_PREV, ch, 2 * NEAR)
            await_rows(send, GRAD_PREV, ch, 2 * NEAR)

        return 0

    lax.fori_loop(0, CHUNKS, drain, 0)


def body(query_rows, key_rows, value_rows, grad_out):
    shape = jax.ShapeDtypeStruct(query_rows.shape, BF16)

    def rows(count, *lead):
        return ((*lead, HEADS, count, DIM), BF16)

    scratch = [
        ((HEADS, 2, SET, DIM), BF16),
        rows(BLOCK),
        rows(BLOCK),
        rows(ONE, 2),
        ((ONE, DIM), BF16),
        ((PLACES, ONE, DIM), BF16),
        ((HEADS, 2, BLOCK, DIM), F32),
        ((HEADS, 2, SET - BLOCK, DIM), BF16),
        rows(2 * BLOCK),
        rows(BLOCK),
        rows(192),
        rows(256),
        rows(ONE),
        rows(BLOCK),
        rows(128),
        rows(256),
        rows(64),
        ((2, HEADS, ONE, DIM), F32),
        ((HEADS, ONE, DIM), F32),
        ((HEADS, 2, 2, NEAR, DIM), BF16),
        ((SET, DIM), F32),
        ((ONE, BLOCK), BF16),
        ((BLOCK, ONE), BF16),
        ((SET, BLOCK), F32),
        ((SET, BLOCK), F32),
        ((2, DIM, BLOCK), F32),
    ]
    anywhere = pl.BlockSpec(memory_space=pl.ANY)
    return pl.pallas_call(
        kernel,
        out_shape=[shape] * 4,
        in_specs=[anywhere] * 4,
        out_specs=[pl.BlockSpec(memory_space=pltpu.VMEM)] * 4,
        scratch_shapes=[pltpu.VMEM(*one) for one in scratch]
        + [pltpu.SemaphoreType.DMA((TRANSFERS, CHUNKS))] * 2
        + [pltpu.SemaphoreType.DMA((1,))] * 2,
        compiler_params=pltpu.CompilerParams(
            collective_id=0, has_side_effects=True, vmem_limit_bytes=58 << 20
        ),
        name="hierarchical",
    )(query_rows, key_rows, value_rows, grad_out)


def solution(mesh):
    placed = P(("grp", "seq"), None)
    return jax.shard_map(
        body, mesh=mesh, in_specs=(placed,) * 4, out_specs=(placed,) * 4, check_vma=False
    )
```

```python
import functools

import jax
import jax.numpy as jnp
from jax import lax
from jax.experimental import pallas as pl
from jax.experimental.pallas import tpu as pltpu
from jax.sharding import PartitionSpec as P

F32 = jnp.float32
BF16 = jnp.bfloat16
HEADS = 8
DIM = 128
BLOCK = 512
NEAR = 256
POOL = 16
ONE = BLOCK // POOL
TWO = ONE // POOL
PLACES = 16
GROUPS = 16
SET = 2048
OWN, PREV, NEXT, LEVEL1, LEVEL2 = 0, 512, 768, 1024, 1536
SCALE = DIM**-0.5
SCALE2 = SCALE * 1.4426950408889634
FILL = -1e30
MESH = pl.DeviceIdType.MESH
CHUNKS = 8
PER = HEADS // CHUNKS
STEP = 512

IN_KV, IN_QG, COLUMN, BESIDE, ALONG, PAIR_SET, FROM_PREV = range(0, 7)
FROM_NEXT, PAIR_GRAD, GRAD_PREV, GRAD_NEXT, ALONG_GRAD, BESIDE_GRAD, COLUMN_GRAD = range(7, 14)
TRANSFERS = 14


def dot_nt(a, b):
    return lax.dot_general(a, b, (((1,), (1,)), ((), ())), preferred_element_type=F32)


def dot_tn(a, b):
    return lax.dot_general(a, b, (((0,), (0,)), ((), ())), preferred_element_type=F32)


def dot_nn(a, b):
    return jnp.dot(a, b, preferred_element_type=F32)


def attend(h, q_all, g_all, kv, bias, att, gq, gown, gset, score, dprob, total):
    query, grad = q_all[h], g_all[h]
    parts = [pl.ds(i * STEP, STEP) for i in range(SET // STEP)]

    def folded(x, op):
        return op(x.reshape(STEP // 8, 8, BLOCK), axis=0)

    top = None
    for rows in parts:
        s = dot_nt(kv[h, 0, rows, :], query)
        b = bias[rows, :]
        s = s + jnp.concatenate([b] * (BLOCK // DIM), axis=1)
        score[rows, :] = s
        part = folded(s, jnp.max)
        top = part if top is None else jnp.maximum(top, part)
    top = jnp.max(top, axis=0, keepdims=True)
    norm = mixed = None
    for rows in parts:
        dp = dot_nt(kv[h, 1, rows, :], grad)
        e = jnp.exp2((score[rows, :] - top) * SCALE2)
        score[rows, :] = e
        dprob[rows, :] = dp
        part, other = folded(e, jnp.sum), folded(e * dp, jnp.sum)
        norm = part if norm is None else norm + part
        mixed = other if mixed is None else mixed + other
    inverse = 1.0 / jnp.sum(norm, axis=0, keepdims=True)
    delta = jnp.sum(mixed, axis=0, keepdims=True) * inverse
    for i, rows in enumerate(parts):
        p = score[rows, :] * inverse
        pb = p.astype(BF16)
        ds = (p * (dprob[rows, :] - delta)).astype(BF16)
        out, dq = dot_tn(kv[h, 1, rows, :], pb), dot_tn(kv[h, 0, rows, :], ds)
        if i == 0:
            total[0], total[1] = out, dq
        else:
            total[0] += out
            total[1] += dq
        dv, dk = dot_nn(pb, grad), dot_nn(ds, query) * SCALE
        if i * STEP < BLOCK:
            gown[h, 0, rows, :] = dk
            gown[h, 1, rows, :] = dv
        else:
            there = pl.ds(i * STEP - BLOCK, STEP)
            gset[h, 0, there, :] = dk.astype(BF16)
            gset[h, 1, there, :] = dv.astype(BF16)
    lanes = pl.ds(pl.multiple_of(h * DIM, DIM), DIM)
    att[:, lanes] = total[0].T.astype(BF16)
    gq[:, lanes] = (total[1].T * SCALE).astype(BF16)


def kernel(
    q_hbm, k_hbm, v_hbm, g_hbm, att, gq, gk, gv,
    kv, q_all, g_all, pooled, told, heard, gown, gset, pair, csend, cin, csum, psend, pin, asend, ain,
    tsend, tin, hrecv, bias, mean, spread, score, dprob, total,
    send, recv, small_send, small_recv,
):
    g, s = lax.axis_index("grp"), lax.axis_index("seq")
    low, z = lax.div(g, 8), lax.rem(g, 8)
    high, x, core = lax.div(s, 8), lax.div(lax.rem(s, 8), 2), lax.rem(s, 2)
    other = 1 - core
    sibling = (g, s + 1 - 2 * core)
    slot_one = x * 4 + high * 2 + core
    has_prev = (g + s) > 0
    has_next = (g + s) < GROUPS + PLACES - 2
    up_group = lax.rem(g + lax.div(s + 1, PLACES), GROUPS)
    after = (up_group, lax.rem(s + 1, PLACES))
    low_group = lax.rem(g + GROUPS - 1 + lax.div(s + PLACES - 1, PLACES), GROUPS)
    before = (low_group, lax.rem(s + PLACES - 1, PLACES))

    def near_x(d):
        return lax.rem(x + d + 4, 4)

    def near_z(d):
        return lax.rem(z + d + 8, 8)

    def beside(d):
        return (g, high * 8 + near_x(d) * 2 + core)

    def along(d):
        return (low * 8 + near_z(d), s)

    def ranks(start, unit, count):
        return pl.ds(pl.multiple_of(start * unit, unit), count)

    def one_rows(column, row, count):
        return ranks(LEVEL1 // ONE + column * 4 + row * 2, ONE, count)

    def two_rows(column, row, count):
        return ranks(LEVEL2 // ONE + column * 2 + row, ONE, count)

    def heads(ch):
        return pl.ds(ch * PER, PER)

    def lanes(h):
        return pl.ds(pl.multiple_of(h * DIM, DIM), DIM)

    def push(transfer, ch, src, dst, device):
        pltpu.make_async_remote_copy(
            src_ref=src, dst_ref=dst, send_sem=send.at[transfer, ch], recv_sem=recv.at[transfer, ch],
            device_id=device, device_id_type=MESH,
        ).start()

    def await_rows(sems, transfer, ch, rows):
        ref = kv.at[heads(ch), 0, pl.ds(0, rows), :]
        pltpu.make_async_copy(ref, ref, sems.at[transfer, ch]).wait()

    def each_head(ch, do):
        lax.fori_loop(0, PER, lambda i, _: (do(ch * PER + i), 0)[1], 0)

    def fetch(h, _):
        ch = lax.div(h, PER)
        for plane, src in enumerate((k_hbm, v_hbm)):
            pltpu.make_async_copy(
                src.at[:, lanes(h)], kv.at[h, plane, pl.ds(OWN, BLOCK), :], recv.at[IN_KV, ch]
            ).start()
        return 0

    def fetch_more(h, _):
        ch = lax.div(h, PER)
        for dst, src in ((q_all, q_hbm), (g_all, g_hbm)):
            pltpu.make_async_copy(src.at[:, lanes(h)], dst.at[h], recv.at[IN_QG, ch]).start()
        return 0

    lax.fori_loop(0, HEADS, fetch, 0)
    lax.fori_loop(0, HEADS, fetch_more, 0)

    barrier = pltpu.get_barrier_semaphore()

    def meet(device):
        pl.semaphore_signal(barrier, inc=1, device_id=device, device_id_type=MESH)

    def column_peer(j):
        rank = lax.rem(low * PLACES + s + j, 2 * PLACES)
        return lax.div(rank, PLACES), lax.rem(rank, PLACES)

    def greet(j, _):
        half, place = column_peer(j)
        meet((half * 8 + z, place))
        return 0

    lax.fori_loop(1, 2 * PLACES, greet, 0)
    lax.fori_loop(1, 8, lambda d, _: (meet(along(d)), 0)[1], 0)
    crosses_up = jnp.logical_and(s == PLACES - 1, has_next)
    crosses_down = jnp.logical_and(s == 0, has_prev)

    @pl.when(crosses_up)
    def _():
        pl.semaphore_signal(barrier, inc=1, device_id=after, device_id_type=MESH)

    @pl.when(crosses_down)
    def _():
        pl.semaphore_signal(barrier, inc=1, device_id=before, device_id_type=MESH)

    wide = (lax.broadcasted_iota(jnp.int32, (ONE, BLOCK), 0), lax.broadcasted_iota(jnp.int32, (ONE, BLOCK), 1))
    mean[...] = jnp.where(lax.shift_right_logical(wide[1], 4) == wide[0], 1.0 / POOL, 0.0).astype(BF16)
    tall = (lax.broadcasted_iota(jnp.int32, (BLOCK, ONE), 0), lax.broadcasted_iota(jnp.int32, (BLOCK, ONE), 1))
    spread[...] = jnp.where(lax.shift_right_logical(tall[0], 4) == tall[1], 1.0 / POOL, 0.0).astype(BF16)

    def pool_own(h, _):
        @pl.when(lax.rem(h, PER) == 0)
        def _():
            await_rows(recv, IN_KV, lax.div(h, PER), 2 * BLOCK)

        for plane in range(2):
            pooled[plane, h] = dot_nn(mean[...], kv[h, plane, pl.ds(OWN, BLOCK), :]).astype(BF16)
        kv[h, core, ranks(LEVEL1 // ONE + slot_one, ONE, ONE), :] = pooled[core, h]
        return 0

    lax.fori_loop(0, HEADS, pool_own, 0)
    told[...] = dot_nn(mean[...], pooled[...].reshape(2 * HEADS * ONE, DIM)).astype(BF16)
    heard[low * PLACES + slot_one] = told[...]

    @pl.when(jnp.logical_not(has_prev))
    def _():
        kv[:, :, PREV:NEXT, :] = jnp.zeros((HEADS, 2, NEAR, DIM), BF16)
        hrecv[:, 0] = jnp.zeros((HEADS, 2, NEAR, DIM), BF16)

    @pl.when(jnp.logical_not(has_next))
    def _():
        kv[:, :, NEXT:LEVEL1, :] = jnp.zeros((HEADS, 2, NEAR, DIM), BF16)
        hrecv[:, 1] = jnp.zeros((HEADS, 2, NEAR, DIM), BF16)

    crosses = jnp.logical_or(crosses_up, crosses_down)

    @pl.when(crosses)
    def _():
        pl.semaphore_wait(barrier, 2 * PLACES - 1 + 7 + 1)

    @pl.when(jnp.logical_not(crosses))
    def _():
        pl.semaphore_wait(barrier, 2 * PLACES - 1 + 7)

    def tell(j, _):
        half, place = column_peer(j)
        pltpu.make_async_remote_copy(
            src_ref=told, dst_ref=heard.at[low * PLACES + slot_one],
            send_sem=small_send.at[0], recv_sem=small_recv.at[0],
            device_id=(half * 8 + z, place), device_id_type=MESH,
        ).start()
        return 0

    lax.fori_loop(1, 2 * PLACES, tell, 0)

    def await_small(sems, which, ref):
        pltpu.make_async_copy(ref, ref, sems.at[which]).wait()

    def spread_rows(v):
        upper = v.astype(BF16)
        rest = (v - upper.astype(F32)).astype(BF16)
        return dot_nn(spread[...], upper) + dot_nn(spread[...], rest)

    def tables():
        row = lax.broadcasted_iota(jnp.int32, (SET, DIM), 0)
        slot = lax.shift_right_logical(row & (BLOCK - 1), 5)
        place = (lax.shift_right_logical(slot, 1) & 1) * 8 + lax.shift_right_logical(slot, 2) * 2 + (slot & 1)
        group = (slot & 1) * 8 + lax.shift_right_logical(slot, 1)
        dead_one = (row >= LEVEL1) & (row < LEVEL2) & (place >= s - 1) & (place <= s + 1)
        dead_two = (row >= LEVEL2) & (group == g)
        no_prev = (row >= PREV) & (row < NEXT) & (g + s == 0)
        no_next = (row >= NEXT) & (row < LEVEL1) & (g + s == GROUPS + PLACES - 2)
        bias[...] = jnp.where(dead_one | dead_two | no_prev | no_next, FILL, 0.0)

    def own_coarse():
        await_small(small_recv, 0, heard.at[pl.ds(0, 2 * PLACES - 1)])
        shape = (HEADS * ONE, PLACES * ONE)
        to, come = lax.broadcasted_iota(jnp.int32, shape, 0), lax.broadcasted_iota(jnp.int32, shape, 1)
        head, within = lax.shift_right_logical(to, 5), to & 31
        wanted = lax.shift_right_logical(within, 1) * ONE + core * 16 + head * 2 + (within & 1)
        pick = jnp.where(come == wanted, 1.0, 0.0).astype(BF16)
        for half in range(2):
            there = heard[half * PLACES : (half + 1) * PLACES].reshape(PLACES * ONE, DIM)
            rows = dot_nn(pick, there).astype(BF16)
            for h in range(HEADS):
                kv[h, core, two_rows(z, half, ONE), :] = rows[h * ONE : (h + 1) * ONE]

    def column(which):
        return (g, (1 - high) * 8 + x * 2 + which)

    def send_column(ch):
        hs = heads(ch)
        mine = ranks(LEVEL1 // ONE + slot_one, ONE, ONE)
        for plane in range(2):
            push(COLUMN, ch, pooled.at[plane, hs], kv.at[hs, plane, mine, :], column(plane))
        push(COLUMN, ch, pooled.at[other, hs], kv.at[hs, other, mine, :], sibling)

    def send_planes(ch):
        hs = heads(ch)
        await_rows(recv, COLUMN, ch, 3 * ONE)
        rows = kv.at[hs, core, one_rows(x, 0, 4 * ONE), :]
        for d in (2, 1, 3):
            push(BESIDE, ch, rows, rows, beside(d))

        @pl.when(ch == 0)
        def _():
            own_coarse()

        both = kv.at[hs, core, two_rows(z, 0, 2 * ONE), :]
        for d in (4, 3, 5, 2, 6, 1, 7):
            push(ALONG, ch, both, both, along(d))

        @pl.when(has_next)
        def _():
            push(FROM_PREV, ch, kv.at[hs, :, pl.ds(OWN + BLOCK - NEAR, NEAR), :], kv.at[hs, :, pl.ds(PREV, NEAR), :], after)

        @pl.when(has_prev)
        def _():
            push(FROM_NEXT, ch, kv.at[hs, :, pl.ds(OWN, NEAR), :], kv.at[hs, :, pl.ds(NEXT, NEAR), :], before)

        @pl.when(ch == 0)
        def _():
            tables()

    def swap_set(ch):
        hs = heads(ch)
        await_rows(recv, BESIDE, ch, 12 * ONE)
        await_rows(recv, ALONG, ch, 14 * ONE)
        whole = kv.at[hs, core, pl.ds(LEVEL1, 2 * BLOCK), :]
        push(PAIR_SET, ch, whole, whole, sibling)

    def compute(ch):
        hs = heads(ch)
        await_rows(recv, IN_QG, ch, 2 * BLOCK)
        await_rows(recv, PAIR_SET, ch, 2 * BLOCK)

        @pl.when(has_prev)
        def _():
            await_rows(recv, FROM_PREV, ch, 2 * NEAR)

        @pl.when(has_next)
        def _():
            await_rows(recv, FROM_NEXT, ch, 2 * NEAR)

        each_head(
            ch,
            lambda h: attend(h, q_all, g_all, kv, bias, att, gq, gown, gset, score, dprob, total),
        )
        push(PAIR_GRAD, ch, gset.at[hs, other, pl.ds(LEVEL1 - BLOCK, 2 * BLOCK), :], pair.at[hs], sibling)

        @pl.when(has_prev)
        def _():
            push(GRAD_NEXT, ch, gset.at[hs, :, pl.ds(PREV - BLOCK, NEAR), :], hrecv.at[hs, 1], before)

        @pl.when(has_next)
        def _():
            push(GRAD_PREV, ch, gset.at[hs, :, pl.ds(NEXT - BLOCK, NEAR), :], hrecv.at[hs, 0], after)

    def added(a, b):
        return (a.astype(F32) + b.astype(F32)).astype(BF16)

    def send_grads(ch):
        hs = heads(ch)
        await_rows(recv, PAIR_GRAD, ch, 2 * BLOCK)

        def add(h):
            psend[h] = added(gset[h, core, pl.ds(LEVEL1 - BLOCK, BLOCK), :], pair[h, pl.ds(0, BLOCK), :])
            csend[h] = added(gset[h, core, pl.ds(LEVEL2 - BLOCK, BLOCK), :], pair[h, pl.ds(BLOCK, BLOCK), :])

        each_head(ch, add)
        for d in (2, 1, 3):
            push(
                BESIDE_GRAD, ch, psend.at[hs, ranks(near_x(d), 128, 128), :],
                pin.at[hs, ranks(x, 128, 128), :], beside(d),
            )
        for d in (4, 3, 5, 2, 6, 1, 7):
            push(
                ALONG_GRAD, ch, csend.at[hs, ranks(near_z(d), 64, 64), :],
                cin.at[hs, ranks(z, 64, 64), :], along(d),
            )

    def column_grads(ch):
        hs = heads(ch)
        await_rows(recv, BESIDE_GRAD, ch, 12 * ONE)

        def add(h):
            v = psend[h, ranks(x, 128, 128), :].astype(F32)
            for d in range(1, 4):
                v = v + pin[h, ranks(near_x(d), 128, 128), :].astype(F32)
            asend[h] = v.astype(BF16)
            ain[h, ranks(core * 2 + high, ONE, ONE), :] = asend[h, ranks(high * 2 + core, ONE, ONE), :]

        each_head(ch, add)
        place = ain.at[hs, ranks(core * 2 + high, ONE, ONE), :]
        for which in range(2):
            push(
                COLUMN_GRAD, ch, asend.at[hs, ranks((1 - high) * 2 + which, ONE, ONE), :], place,
                column(which),
            )
        push(COLUMN_GRAD, ch, asend.at[hs, ranks(high * 2 + other, ONE, ONE), :], place, sibling)
        await_rows(recv, ALONG_GRAD, ch, 14 * ONE)

        def add_coarse(h):
            v = csend[h, ranks(z, 64, 64), :].astype(F32)
            for d in range(1, 8):
                v = v + cin[h, ranks(near_z(d), 64, 64), :].astype(F32)
            csum[h] = v.astype(BF16)

        each_head(ch, add_coarse)

    def finish(ch):
        await_rows(recv, COLUMN_GRAD, ch, 3 * ONE)

        @pl.when(has_prev)
        def _():
            await_rows(recv, GRAD_PREV, ch, 2 * NEAR)

        @pl.when(has_next)
        def _():
            await_rows(recv, GRAD_NEXT, ch, 2 * NEAR)

        def add(h):
            for plane in range(2):
                level = ain[h, pl.ds(2 * plane * ONE, ONE), :].astype(F32)
                level = level + ain[h, pl.ds((2 * plane + 1) * ONE, ONE), :].astype(F32)
                sums = gown[h, plane] + spread_rows(level)
                for side in range(2):
                    rows = slice(side * NEAR, (side + 1) * NEAR)
                    gown[h, plane, rows, :] = sums[rows] + hrecv[h, side, plane].astype(F32)

        each_head(ch, add)

    stages = (send_column, send_planes, swap_set, compute, send_grads, column_grads, finish)

    def step(t, _):
        for lag, stage in enumerate(stages):
            pl.when(jnp.logical_and(t >= lag, t < CHUNKS + lag))(functools.partial(stage, t - lag))

        @pl.when(t == CHUNKS + 4)
        def _():
            send_coarse_sums()

        return 0

    def send_coarse_sums():
        shape = (BLOCK, BLOCK)
        to, come = lax.broadcasted_iota(jnp.int32, shape, 0), lax.broadcasted_iota(jnp.int32, shape, 1)
        target, within = lax.shift_right_logical(to, 4), to & 15
        wanted = lax.shift_right_logical(within, 1) * 64 + target * 2 + (within & 1)
        pick = jnp.where(come == wanted, 1.0, 0.0).astype(BF16)
        tsend[...] = dot_nn(pick, csum[...].reshape(BLOCK, DIM)).astype(BF16)
        source = low * 8 + high * 4 + x
        tin[core, source] = tsend[ranks(low * PLACES + slot_one, 16, 16), :]

        def tell_sums(j, _):
            half, place = column_peer(j)
            slot = lax.div(lax.rem(place, 8), 2) * 4 + lax.div(place, 8) * 2 + lax.rem(place, 2)
            pltpu.make_async_remote_copy(
                src_ref=tsend.at[ranks(half * PLACES + slot, 16, 16), :], dst_ref=tin.at[core, source],
                send_sem=small_send.at[1], recv_sem=small_recv.at[1],
                device_id=(half * 8 + z, place), device_id_type=MESH,
            ).start()
            return 0

        lax.fori_loop(1, 2 * PLACES, tell_sums, 0)

    lax.fori_loop(0, CHUNKS + len(stages) - 1, step, 0)

    sums_in = tsend.at[pl.ds(0, (2 * PLACES - 1) * 16), :]
    await_small(small_recv, 1, sums_in)
    for plane, dst in enumerate((gk, gv)):
        coarse = tin[plane, 0].astype(F32)
        for i in range(1, 16):
            coarse = coarse + tin[plane, i].astype(F32)
        coarse = coarse * (1.0 / (POOL * POOL))
        for h in range(HEADS):
            for side in range(2):
                rows = slice(side * NEAR, (side + 1) * NEAR)
                row = coarse[2 * h + side : 2 * h + side + 1]
                dst[rows, h * DIM : (h + 1) * DIM] = (gown[h, plane, rows, :] + row).astype(BF16)

    await_small(small_send, 0, heard.at[pl.ds(0, 2 * PLACES - 1)])
    await_small(small_send, 1, sums_in)

    def drain(ch, _):
        for transfer, rows in (
            (COLUMN, 96), (BESIDE, 384), (ALONG, 448), (PAIR_SET, 1024),
            (PAIR_GRAD, 1024), (ALONG_GRAD, 448), (BESIDE_GRAD, 384), (COLUMN_GRAD, 96),
        ):
            await_rows(send, transfer, ch, rows)

        @pl.when(has_prev)
        def _():
            await_rows(send, FROM_NEXT, ch, 2 * NEAR)
            await_rows(send, GRAD_NEXT, ch, 2 * NEAR)

        @pl.when(has_next)
        def _():
            await_rows(send, FROM_PREV, ch, 2 * NEAR)
            await_rows(send, GRAD_PREV, ch, 2 * NEAR)

        return 0

    lax.fori_loop(0, CHUNKS, drain, 0)


def body(query_rows, key_rows, value_rows, grad_out):
    shape = jax.ShapeDtypeStruct(query_rows.shape, BF16)

    def rows(count, *lead):
        return ((*lead, HEADS, count, DIM), BF16)

    scratch = [
        ((HEADS, 2, SET, DIM), BF16),
        rows(BLOCK),
        rows(BLOCK),
        rows(ONE, 2),
        ((ONE, DIM), BF16),
        ((2 * PLACES, ONE, DIM), BF16),
        ((HEADS, 2, BLOCK, DIM), F32),
        ((HEADS, 2, SET - BLOCK, DIM), BF16),
        rows(2 * BLOCK),
        rows(BLOCK),
        rows(BLOCK),
        rows(64),
        rows(BLOCK),
        rows(BLOCK),
        rows(128),
        rows(128),
        ((BLOCK, DIM), BF16),
        ((2, 16, 16, DIM), BF16),
        ((HEADS, 2, 2, NEAR, DIM), BF16),
        ((SET, DIM), F32),
        ((ONE, BLOCK), BF16),
        ((BLOCK, ONE), BF16),
        ((SET, BLOCK), F32),
        ((SET, BLOCK), F32),
        ((2, DIM, BLOCK), F32),
    ]
    anywhere = pl.BlockSpec(memory_space=pl.ANY)
    return pl.pallas_call(
        kernel,
        out_shape=[shape] * 4,
        in_specs=[anywhere] * 4,
        out_specs=[pl.BlockSpec(memory_space=pltpu.VMEM)] * 4,
        scratch_shapes=[pltpu.VMEM(*one) for one in scratch]
        + [pltpu.SemaphoreType.DMA((TRANSFERS, CHUNKS))] * 2
        + [pltpu.SemaphoreType.DMA((2,))] * 2,
        compiler_params=pltpu.CompilerParams(
            collective_id=0, has_side_effects=True, vmem_limit_bytes=58 << 20
        ),
        name="hierarchical",
    )(query_rows, key_rows, value_rows, grad_out)


def solution(mesh):
    placed = P(("grp", "seq"), None)
    return jax.shard_map(
        body, mesh=mesh, in_specs=(placed,) * 4, out_specs=(placed,) * 4, check_vma=False
    )
```

```python
import functools

import jax
import jax.numpy as jnp
from jax import lax
from jax.experimental import pallas as pl
from jax.experimental.pallas import tpu as pltpu
from jax.sharding import PartitionSpec as P

F32 = jnp.float32
BF16 = jnp.bfloat16
HEADS = 8
DIM = 128
BLOCK = 512
NEAR = 256
POOL = 16
ONE = BLOCK // POOL
TWO = ONE // POOL
PLACES = 16
GROUPS = 16
SET = 2048
OWN, PREV, NEXT, LEVEL1, LEVEL2 = 0, 512, 768, 1024, 1536
SCALE = DIM**-0.5
SCALE2 = SCALE * 1.4426950408889634
FILL = -1e30
MESH = pl.DeviceIdType.MESH
CHUNKS = 8
PER = 1
STEP = 512

IN_KV, IN_QG, COLUMN, BESIDE, ALONG, ACROSS, PAIR_SET, FROM_PREV = range(0, 8)
FROM_NEXT, PAIR_GRAD, GRAD_PREV, GRAD_NEXT, ALONG_GRAD, ACROSS_GRAD, BESIDE_GRAD, COLUMN_GRAD = range(8, 16)
TRANSFERS = 16
FORWARD = (IN_KV, IN_QG, COLUMN, BESIDE, ALONG, ACROSS, PAIR_SET, FROM_PREV, FROM_NEXT)
PER_IN = 2
LOADS = HEADS // PER_IN


def dot_nt(a, b):
    return lax.dot_general(a, b, (((1,), (1,)), ((), ())), preferred_element_type=F32)


def dot_tn(a, b):
    return lax.dot_general(a, b, (((0,), (0,)), ((), ())), preferred_element_type=F32)


def dot_nn(a, b):
    return jnp.dot(a, b, preferred_element_type=F32)


def attend(h, q_all, g_all, kv, bias, att, gq, gown, gset, score, dprob, total):
    query, grad = q_all[h], g_all[h]
    parts = [pl.ds(i * STEP, STEP) for i in range(SET // STEP)]

    def folded(x, op):
        return op(x.reshape(STEP // 8, 8, BLOCK), axis=0)

    top = None
    for rows in parts:
        s = dot_nt(kv[h, 0, rows, :], query)
        b = bias[rows, :]
        s = s + jnp.concatenate([b] * (BLOCK // DIM), axis=1)
        score[rows, :] = s
        part = folded(s, jnp.max)
        top = part if top is None else jnp.maximum(top, part)
    top = jnp.max(top, axis=0, keepdims=True)
    norm = mixed = None
    for rows in parts:
        dp = dot_nt(kv[h, 1, rows, :], grad)
        e = jnp.exp2((score[rows, :] - top) * SCALE2)
        score[rows, :] = e
        dprob[rows, :] = dp
        part, other = folded(e, jnp.sum), folded(e * dp, jnp.sum)
        norm = part if norm is None else norm + part
        mixed = other if mixed is None else mixed + other
    inverse = 1.0 / jnp.sum(norm, axis=0, keepdims=True)
    delta = jnp.sum(mixed, axis=0, keepdims=True) * inverse
    for i, rows in enumerate(parts):
        p = score[rows, :] * inverse
        pb = p.astype(BF16)
        ds = (p * (dprob[rows, :] - delta)).astype(BF16)
        out, dq = dot_tn(kv[h, 1, rows, :], pb), dot_tn(kv[h, 0, rows, :], ds)
        if i == 0:
            total[0], total[1] = out, dq
        else:
            total[0] += out
            total[1] += dq
        dv, dk = dot_nn(pb, grad), dot_nn(ds, query) * SCALE
        if i * STEP < BLOCK:
            gown[h, 0, rows, :] = dk
            gown[h, 1, rows, :] = dv
        else:
            there = pl.ds(i * STEP - BLOCK, STEP)
            gset[h, 0, there, :] = dk.astype(BF16)
            gset[h, 1, there, :] = dv.astype(BF16)
    lanes = pl.ds(pl.multiple_of(h * DIM, DIM), DIM)
    att[:, lanes] = total[0].T.astype(BF16)
    gq[:, lanes] = (total[1].T * SCALE).astype(BF16)


def kernel(
    q_hbm, k_hbm, v_hbm, g_hbm, att, gq, gk, gv,
    kv, q_all, g_all, pooled, told, heard, gown, gset, pair, csend, clow, cline, cin, csum, psend, pin, asend, ain,
    tsend, tin, hrecv, bias, mean, spread, score, dprob, total,
    send, recv, small_send, small_recv,
):
    g, s = lax.axis_index("grp"), lax.axis_index("seq")
    low, z = lax.div(g, 8), lax.rem(g, 8)
    high, x, core = lax.div(s, 8), lax.div(lax.rem(s, 8), 2), lax.rem(s, 2)
    other = 1 - core
    sibling = (g, s + 1 - 2 * core)
    slot_one = x * 4 + high * 2 + core
    across = ((1 - low) * 8 + z, s)
    has_prev = (g + s) > 0
    has_next = (g + s) < GROUPS + PLACES - 2
    up_group = lax.rem(g + lax.div(s + 1, PLACES), GROUPS)
    after = (up_group, lax.rem(s + 1, PLACES))
    low_group = lax.rem(g + GROUPS - 1 + lax.div(s + PLACES - 1, PLACES), GROUPS)
    before = (low_group, lax.rem(s + PLACES - 1, PLACES))

    def near_x(d):
        return lax.rem(x + d + 4, 4)

    def near_z(d):
        return lax.rem(z + d + 8, 8)

    def beside(d):
        return (g, high * 8 + near_x(d) * 2 + core)

    def along(d):
        return (low * 8 + near_z(d), s)

    def ranks(start, unit, count):
        return pl.ds(pl.multiple_of(start * unit, unit), count)

    def one_rows(column, row, count):
        return ranks(LEVEL1 // ONE + column * 4 + row * 2, ONE, count)

    def two_rows(group, count):
        return ranks(LEVEL2 // ONE + group, ONE, count)

    def loads(ch):
        return pl.ds(ch * PER_IN, PER_IN)

    def heads(ch):
        return pl.ds(ch * PER, PER)

    def lanes(h):
        return pl.ds(pl.multiple_of(h * DIM, DIM), DIM)

    def push(transfer, ch, src, dst, device):
        pltpu.make_async_remote_copy(
            src_ref=src, dst_ref=dst, send_sem=send.at[transfer, ch], recv_sem=recv.at[transfer, ch],
            device_id=device, device_id_type=MESH,
        ).start()

    def await_rows(sems, transfer, ch, rows):
        ref = kv.at[loads(ch) if transfer in FORWARD else heads(ch), 0, pl.ds(0, rows), :]
        pltpu.make_async_copy(ref, ref, sems.at[transfer, ch]).wait()

    def each_head(ch, do):
        lax.fori_loop(0, PER, lambda i, _: (do(ch * PER + i), 0)[1], 0)

    def fetch(h, _):
        ch = lax.div(h, PER_IN)
        for plane, src in enumerate((k_hbm, v_hbm)):
            pltpu.make_async_copy(
                src.at[:, lanes(h)], kv.at[h, plane, pl.ds(OWN, BLOCK), :], recv.at[IN_KV, ch]
            ).start()
        return 0

    def fetch_more(h, _):
        ch = lax.div(h, PER_IN)
        for dst, src in ((q_all, q_hbm), (g_all, g_hbm)):
            pltpu.make_async_copy(src.at[:, lanes(h)], dst.at[h], recv.at[IN_QG, ch]).start()
        return 0

    lax.fori_loop(0, HEADS, fetch, 0)
    lax.fori_loop(0, HEADS, fetch_more, 0)

    barrier = pltpu.get_barrier_semaphore()

    def meet(device):
        pl.semaphore_signal(barrier, inc=1, device_id=device, device_id_type=MESH)

    lax.fori_loop(1, PLACES, lambda j, _: (meet((g, lax.rem(s + j, PLACES))), 0)[1], 0)
    lax.fori_loop(1, 8, lambda d, _: (meet(along(d)), 0)[1], 0)
    meet(across)
    crosses_up = jnp.logical_and(s == PLACES - 1, has_next)
    crosses_down = jnp.logical_and(s == 0, has_prev)

    @pl.when(crosses_up)
    def _():
        pl.semaphore_signal(barrier, inc=1, device_id=after, device_id_type=MESH)

    @pl.when(crosses_down)
    def _():
        pl.semaphore_signal(barrier, inc=1, device_id=before, device_id_type=MESH)

    wide = (lax.broadcasted_iota(jnp.int32, (ONE, BLOCK), 0), lax.broadcasted_iota(jnp.int32, (ONE, BLOCK), 1))
    mean[...] = jnp.where(lax.shift_right_logical(wide[1], 4) == wide[0], 1.0 / POOL, 0.0).astype(BF16)
    tall = (lax.broadcasted_iota(jnp.int32, (BLOCK, ONE), 0), lax.broadcasted_iota(jnp.int32, (BLOCK, ONE), 1))
    spread[...] = jnp.where(lax.shift_right_logical(tall[0], 4) == tall[1], 1.0 / POOL, 0.0).astype(BF16)

    def pool_own(h, _):
        @pl.when(lax.rem(h, PER_IN) == 0)
        def _():
            await_rows(recv, IN_KV, lax.div(h, PER_IN), 2 * BLOCK)

        for plane in range(2):
            pooled[plane, h] = dot_nn(mean[...], kv[h, plane, pl.ds(OWN, BLOCK), :]).astype(BF16)
        kv[h, core, ranks(LEVEL1 // ONE + slot_one, ONE, ONE), :] = pooled[core, h]
        return 0

    lax.fori_loop(0, HEADS, pool_own, 0)
    told[...] = dot_nn(mean[...], pooled[...].reshape(2 * HEADS * ONE, DIM)).astype(BF16)
    heard[slot_one] = told[...]

    @pl.when(jnp.logical_not(has_prev))
    def _():
        kv[:, :, PREV:NEXT, :] = jnp.zeros((HEADS, 2, NEAR, DIM), BF16)
        hrecv[:, 0] = jnp.zeros((HEADS, 2, NEAR, DIM), BF16)

    @pl.when(jnp.logical_not(has_next))
    def _():
        kv[:, :, NEXT:LEVEL1, :] = jnp.zeros((HEADS, 2, NEAR, DIM), BF16)
        hrecv[:, 1] = jnp.zeros((HEADS, 2, NEAR, DIM), BF16)

    crosses = jnp.logical_or(crosses_up, crosses_down)

    @pl.when(crosses)
    def _():
        pl.semaphore_wait(barrier, PLACES - 1 + 8 + 1)

    @pl.when(jnp.logical_not(crosses))
    def _():
        pl.semaphore_wait(barrier, PLACES - 1 + 8)

    def tell(j, _):
        pltpu.make_async_remote_copy(
            src_ref=told, dst_ref=heard.at[slot_one],
            send_sem=small_send.at[0], recv_sem=small_recv.at[0],
            device_id=(g, lax.rem(s + j, PLACES)), device_id_type=MESH,
        ).start()
        return 0

    lax.fori_loop(1, PLACES, tell, 0)

    def await_small(sems, which, ref):
        pltpu.make_async_copy(ref, ref, sems.at[which]).wait()

    def spread_rows(v):
        upper = v.astype(BF16)
        rest = (v - upper.astype(F32)).astype(BF16)
        return dot_nn(spread[...], upper) + dot_nn(spread[...], rest)

    def tables():
        row = lax.broadcasted_iota(jnp.int32, (SET, DIM), 0)
        slot = lax.shift_right_logical(row & (BLOCK - 1), 5)
        place = (lax.shift_right_logical(slot, 1) & 1) * 8 + lax.shift_right_logical(slot, 2) * 2 + (slot & 1)
        dead_one = (row >= LEVEL1) & (row < LEVEL2) & (place >= s - 1) & (place <= s + 1)
        dead_two = (row >= LEVEL2) & (slot == g)
        no_prev = (row >= PREV) & (row < NEXT) & (g + s == 0)
        no_next = (row >= NEXT) & (row < LEVEL1) & (g + s == GROUPS + PLACES - 2)
        bias[...] = jnp.where(dead_one | dead_two | no_prev | no_next, FILL, 0.0)

    def own_coarse():
        await_small(small_recv, 0, heard.at[pl.ds(0, PLACES - 1)])
        shape = (HEADS * ONE, PLACES * ONE)
        to, come = lax.broadcasted_iota(jnp.int32, shape, 0), lax.broadcasted_iota(jnp.int32, shape, 1)
        head, within = lax.shift_right_logical(to, 5), to & 31
        wanted = lax.shift_right_logical(within, 1) * ONE + core * 16 + head * 2 + (within & 1)
        pick = jnp.where(come == wanted, 1.0, 0.0).astype(BF16)
        rows = dot_nn(pick, heard[...].reshape(PLACES * ONE, DIM)).astype(BF16)
        for h in range(HEADS):
            kv[h, core, two_rows(g, ONE), :] = rows[h * ONE : (h + 1) * ONE]

    def column(which):
        return (g, (1 - high) * 8 + x * 2 + which)

    def send_column(ch):
        hs = loads(ch)
        mine = ranks(LEVEL1 // ONE + slot_one, ONE, ONE)
        for plane in range(2):
            push(COLUMN, ch, pooled.at[plane, hs], kv.at[hs, plane, mine, :], column(plane))
        push(COLUMN, ch, pooled.at[other, hs], kv.at[hs, other, mine, :], sibling)

    def send_planes(ch):
        hs = loads(ch)
        await_rows(recv, COLUMN, ch, 3 * ONE)
        rows = kv.at[hs, core, one_rows(x, 0, 4 * ONE), :]
        for d in (2, 1, 3):
            push(BESIDE, ch, rows, rows, beside(d))

        @pl.when(ch == 0)
        def _():
            own_coarse()

        group = kv.at[hs, core, two_rows(g, ONE), :]
        for d in (4, 3, 5, 2, 6, 1, 7):
            push(ALONG, ch, group, group, along(d))

        @pl.when(has_next)
        def _():
            push(FROM_PREV, ch, kv.at[hs, :, pl.ds(OWN + BLOCK - NEAR, NEAR), :], kv.at[hs, :, pl.ds(PREV, NEAR), :], after)

        @pl.when(has_prev)
        def _():
            push(FROM_NEXT, ch, kv.at[hs, :, pl.ds(OWN, NEAR), :], kv.at[hs, :, pl.ds(NEXT, NEAR), :], before)

        @pl.when(ch == 0)
        def _():
            tables()

    def send_across(ch):
        hs = loads(ch)
        await_rows(recv, ALONG, ch, 7 * ONE)
        line = kv.at[hs, core, two_rows(low * 8, 8 * ONE), :]
        push(ACROSS, ch, line, line, across)

    def swap_set(ch):
        hs = loads(ch)
        await_rows(recv, BESIDE, ch, 12 * ONE)
        await_rows(recv, ACROSS, ch, 8 * ONE)
        whole = kv.at[hs, core, pl.ds(LEVEL1, 2 * BLOCK), :]
        push(PAIR_SET, ch, whole, whole, sibling)

    def await_set(ch):
        await_rows(recv, IN_QG, ch, 2 * BLOCK)
        await_rows(recv, PAIR_SET, ch, 2 * BLOCK)

        @pl.when(has_prev)
        def _():
            await_rows(recv, FROM_PREV, ch, 2 * NEAR)

        @pl.when(has_next)
        def _():
            await_rows(recv, FROM_NEXT, ch, 2 * NEAR)

    def compute(ch):
        hs = heads(ch)
        ready = lax.div(ch, PER_IN)
        pl.when(lax.rem(ch, PER_IN) == 0)(functools.partial(await_set, ready))
        each_head(
            ch,
            lambda h: attend(h, q_all, g_all, kv, bias, att, gq, gown, gset, score, dprob, total),
        )
        push(PAIR_GRAD, ch, gset.at[hs, other, pl.ds(LEVEL1 - BLOCK, 2 * BLOCK), :], pair.at[hs], sibling)

        @pl.when(has_prev)
        def _():
            push(GRAD_NEXT, ch, gset.at[hs, :, pl.ds(PREV - BLOCK, NEAR), :], hrecv.at[hs, 1], before)

        @pl.when(has_next)
        def _():
            push(GRAD_PREV, ch, gset.at[hs, :, pl.ds(NEXT - BLOCK, NEAR), :], hrecv.at[hs, 0], after)

    def added(a, b):
        return (a.astype(F32) + b.astype(F32)).astype(BF16)

    def send_grads(ch):
        hs = heads(ch)
        await_rows(recv, PAIR_GRAD, ch, 2 * BLOCK)

        def add(h):
            psend[h] = added(gset[h, core, pl.ds(LEVEL1 - BLOCK, BLOCK), :], pair[h, pl.ds(0, BLOCK), :])
            csend[h] = added(gset[h, core, pl.ds(LEVEL2 - BLOCK, BLOCK), :], pair[h, pl.ds(BLOCK, BLOCK), :])

        each_head(ch, add)
        for d in (2, 1, 3):
            push(
                BESIDE_GRAD, ch, psend.at[hs, ranks(near_x(d), 128, 128), :],
                pin.at[hs, ranks(x, 128, 128), :], beside(d),
            )
        push(
            ACROSS_GRAD, ch, csend.at[hs, ranks((1 - low) * 8, ONE, 8 * ONE), :], clow.at[hs], across,
        )

    def column_grads(ch):
        hs = heads(ch)
        await_rows(recv, BESIDE_GRAD, ch, 12 * ONE)

        def add(h):
            v = psend[h, ranks(x, 128, 128), :].astype(F32)
            for d in range(1, 4):
                v = v + pin[h, ranks(near_x(d), 128, 128), :].astype(F32)
            asend[h] = v.astype(BF16)
            ain[h, ranks(core * 2 + high, ONE, ONE), :] = asend[h, ranks(high * 2 + core, ONE, ONE), :]

        each_head(ch, add)
        place = ain.at[hs, ranks(core * 2 + high, ONE, ONE), :]
        for which in range(2):
            push(
                COLUMN_GRAD, ch, asend.at[hs, ranks((1 - high) * 2 + which, ONE, ONE), :], place,
                column(which),
            )
        push(COLUMN_GRAD, ch, asend.at[hs, ranks(high * 2 + other, ONE, ONE), :], place, sibling)
        await_rows(recv, ACROSS_GRAD, ch, 8 * ONE)

        def add_line(h):
            cline[h] = added(csend[h, ranks(low * 8, ONE, 8 * ONE), :], clow[h])

        each_head(ch, add_line)
        for d in (4, 3, 5, 2, 6, 1, 7):
            push(
                ALONG_GRAD, ch, cline.at[hs, ranks(near_z(d), ONE, ONE), :],
                cin.at[hs, ranks(z, ONE, ONE), :], along(d),
            )

    def coarse_sums(ch):
        await_rows(recv, ALONG_GRAD, ch, 7 * ONE)

        def add(h):
            v = cline[h, ranks(z, ONE, ONE), :].astype(F32)
            for d in range(1, 8):
                v = v + cin[h, ranks(near_z(d), ONE, ONE), :].astype(F32)
            csum[h] = v.astype(BF16)

        each_head(ch, add)

    def finish(ch):
        await_rows(recv, COLUMN_GRAD, ch, 3 * ONE)

        @pl.when(has_prev)
        def _():
            await_rows(recv, GRAD_PREV, ch, 2 * NEAR)

        @pl.when(has_next)
        def _():
            await_rows(recv, GRAD_NEXT, ch, 2 * NEAR)

        def add(h):
            for plane in range(2):
                level = ain[h, pl.ds(2 * plane * ONE, ONE), :].astype(F32)
                level = level + ain[h, pl.ds((2 * plane + 1) * ONE, ONE), :].astype(F32)
                sums = gown[h, plane] + spread_rows(level)
                for side in range(2):
                    rows = slice(side * NEAR, (side + 1) * NEAR)
                    gown[h, plane, rows, :] = sums[rows] + hrecv[h, side, plane].astype(F32)

        each_head(ch, add)

    inward = (send_column, send_planes, send_across, swap_set)
    outward = (compute, send_grads, column_grads, coarse_sums, finish)
    lead = len(inward) - 1

    def step(t, _):
        for lag, stage in enumerate(inward):
            pl.when(jnp.logical_and(t >= lag, t < LOADS + lag))(functools.partial(stage, t - lag))
        for i, stage in enumerate(outward):
            lag = lead + 1 + i
            pl.when(jnp.logical_and(t >= lag, t < CHUNKS + lag))(functools.partial(stage, t - lag))
            if stage is coarse_sums:
                pl.when(t == CHUNKS + lag - 1)(send_coarse_sums)
        return 0

    def send_coarse_sums():
        shape = (HEADS * ONE, HEADS * ONE)
        to, come = lax.broadcasted_iota(jnp.int32, shape, 0), lax.broadcasted_iota(jnp.int32, shape, 1)
        target, within = lax.shift_right_logical(to, 4), to & 15
        wanted = lax.shift_right_logical(within, 1) * ONE + target * 2 + (within & 1)
        pick = jnp.where(come == wanted, 1.0, 0.0).astype(BF16)
        tsend[...] = dot_nn(pick, csum[...].reshape(HEADS * ONE, DIM)).astype(BF16)
        source = high * 4 + x
        tin[core, source] = tsend[ranks(slot_one, 16, 16), :]

        def tell_sums(j, _):
            place = lax.rem(s + j, PLACES)
            slot = lax.div(lax.rem(place, 8), 2) * 4 + lax.div(place, 8) * 2 + lax.rem(place, 2)
            pltpu.make_async_remote_copy(
                src_ref=tsend.at[ranks(slot, 16, 16), :], dst_ref=tin.at[core, source],
                send_sem=small_send.at[1], recv_sem=small_recv.at[1],
                device_id=(g, place), device_id_type=MESH,
            ).start()
            return 0

        lax.fori_loop(1, PLACES, tell_sums, 0)

    lax.fori_loop(0, CHUNKS + lead + len(outward), step, 0)

    sums_in = tsend.at[pl.ds(0, (PLACES - 1) * 16), :]
    await_small(small_recv, 1, sums_in)
    for plane, dst in enumerate((gk, gv)):
        coarse = tin[plane, 0].astype(F32)
        for i in range(1, 8):
            coarse = coarse + tin[plane, i].astype(F32)
        coarse = coarse * (1.0 / (POOL * POOL))
        for h in range(HEADS):
            for side in range(2):
                rows = slice(side * NEAR, (side + 1) * NEAR)
                row = coarse[2 * h + side : 2 * h + side + 1]
                dst[rows, h * DIM : (h + 1) * DIM] = (gown[h, plane, rows, :] + row).astype(BF16)

    await_small(small_send, 0, heard.at[pl.ds(0, PLACES - 1)])
    await_small(small_send, 1, sums_in)

    def drain(ch, _):
        for transfer, rows in (
            (PAIR_GRAD, 1024), (ACROSS_GRAD, 256), (ALONG_GRAD, 224), (BESIDE_GRAD, 384), (COLUMN_GRAD, 96),
        ):
            await_rows(send, transfer, ch, rows)
        pl.when(has_prev)(lambda: await_rows(send, GRAD_NEXT, ch, 2 * NEAR))
        pl.when(has_next)(lambda: await_rows(send, GRAD_PREV, ch, 2 * NEAR))
        return 0

    def drain_in(ch, _):
        for transfer, rows in ((COLUMN, 96), (BESIDE, 384), (ALONG, 224), (ACROSS, 256), (PAIR_SET, 1024)):
            await_rows(send, transfer, ch, rows)
        pl.when(has_prev)(lambda: await_rows(send, FROM_NEXT, ch, 2 * NEAR))
        pl.when(has_next)(lambda: await_rows(send, FROM_PREV, ch, 2 * NEAR))
        return 0

    lax.fori_loop(0, LOADS, drain_in, 0)
    lax.fori_loop(0, CHUNKS, drain, 0)


def body(query_rows, key_rows, value_rows, grad_out):
    shape = pltpu.VMEM(query_rows.shape, BF16)

    def rows(count, *lead):
        return ((*lead, HEADS, count, DIM), BF16)

    scratch = [
        ((HEADS, 2, SET, DIM), BF16),
        rows(BLOCK),
        rows(BLOCK),
        rows(ONE, 2),
        ((ONE, DIM), BF16),
        ((PLACES, ONE, DIM), BF16),
        ((HEADS, 2, BLOCK, DIM), F32),
        ((HEADS, 2, SET - BLOCK, DIM), BF16),
        rows(2 * BLOCK),
        rows(BLOCK),
        rows(8 * ONE),
        rows(8 * ONE),
        rows(8 * ONE),
        rows(ONE),
        rows(BLOCK),
        rows(BLOCK),
        rows(128),
        rows(128),
        ((HEADS * ONE, DIM), BF16),
        ((2, 8, 16, DIM), BF16),
        ((HEADS, 2, 2, NEAR, DIM), BF16),
        ((SET, DIM), F32),
        ((ONE, BLOCK), BF16),
        ((BLOCK, ONE), BF16),
        ((SET, BLOCK), F32),
        ((SET, BLOCK), F32),
        ((2, DIM, BLOCK), F32),
    ]
    anywhere = pl.BlockSpec(memory_space=pl.ANY)
    return pl.pallas_call(
        kernel,
        out_shape=[shape] * 4,
        in_specs=[anywhere] * 4,
        out_specs=[pl.BlockSpec(memory_space=pltpu.VMEM)] * 4,
        scratch_shapes=[pltpu.VMEM(*one) for one in scratch]
        + [pltpu.SemaphoreType.DMA((TRANSFERS, CHUNKS))] * 2
        + [pltpu.SemaphoreType.DMA((2,))] * 2,
        compiler_params=pltpu.CompilerParams(
            collective_id=0, has_side_effects=True, vmem_limit_bytes=50 << 20
        ),
        name="hierarchical",
    )(query_rows, key_rows, value_rows, grad_out)


def solution(mesh):
    placed = P(("grp", "seq"), None)
    return jax.shard_map(
        body, mesh=mesh, in_specs=(placed,) * 4, out_specs=(placed,) * 4, check_vma=False
    )
```

```python
import functools

import jax
import jax.numpy as jnp
from jax import lax
from jax.experimental import pallas as pl
from jax.experimental.pallas import tpu as pltpu
from jax.sharding import PartitionSpec as P

F32 = jnp.float32
BF16 = jnp.bfloat16
HEADS = 8
DIM = 128
BLOCK = 512
NEAR = 256
POOL = 16
ONE = BLOCK // POOL
TWO = ONE // POOL
PLACES = 16
GROUPS = 16
SET = 2048
OWN, PREV, NEXT, LEVEL1, LEVEL2 = 0, 512, 768, 1024, 1536
SCALE = DIM**-0.5
SCALE2 = SCALE * 1.4426950408889634
FILL = -1e30
MESH = pl.DeviceIdType.MESH
CHUNKS = 8
PER = 1
STEP = 512

IN_KV, IN_QG, COLUMN, BESIDE, ALONG, ACROSS, PAIR_SET, FROM_PREV = range(0, 8)
FROM_NEXT, PAIR_GRAD, GRAD_PREV, GRAD_NEXT, ALONG_GRAD, ACROSS_GRAD, BESIDE_GRAD, COLUMN_GRAD = range(8, 16)
TRANSFERS = 16
FORWARD = (IN_KV, IN_QG, COLUMN, BESIDE, ALONG, ACROSS, PAIR_SET, FROM_PREV, FROM_NEXT)
PER_IN = 1
LOADS = HEADS // PER_IN


def dot_nt(a, b):
    return lax.dot_general(a, b, (((1,), (1,)), ((), ())), preferred_element_type=F32)


def dot_tn(a, b):
    return lax.dot_general(a, b, (((0,), (0,)), ((), ())), preferred_element_type=F32)


def dot_nn(a, b):
    return jnp.dot(a, b, preferred_element_type=F32)


def attend(h, q_all, g_all, kv, bias, att, gq, gown, gset, score, dprob, total):
    query, grad = q_all[h], g_all[h]
    parts = [pl.ds(i * STEP, STEP) for i in range(SET // STEP)]

    def folded(x, op):
        return op(x.reshape(STEP // 8, 8, BLOCK), axis=0)

    top = None
    for rows in parts:
        s = dot_nt(kv[h, 0, rows, :], query)
        b = bias[rows, :]
        s = s + jnp.concatenate([b] * (BLOCK // DIM), axis=1)
        score[rows, :] = s
        part = folded(s, jnp.max)
        top = part if top is None else jnp.maximum(top, part)
    top = jnp.max(top, axis=0, keepdims=True)
    norm = mixed = None
    for rows in parts:
        dp = dot_nt(kv[h, 1, rows, :], grad)
        e = jnp.exp2((score[rows, :] - top) * SCALE2)
        score[rows, :] = e
        dprob[rows, :] = dp
        part, other = folded(e, jnp.sum), folded(e * dp, jnp.sum)
        norm = part if norm is None else norm + part
        mixed = other if mixed is None else mixed + other
    inverse = 1.0 / jnp.sum(norm, axis=0, keepdims=True)
    delta = jnp.sum(mixed, axis=0, keepdims=True) * inverse
    for i, rows in enumerate(parts):
        p = score[rows, :] * inverse
        pb = p.astype(BF16)
        ds = (p * (dprob[rows, :] - delta)).astype(BF16)
        out, dq = dot_tn(kv[h, 1, rows, :], pb), dot_tn(kv[h, 0, rows, :], ds)
        if i == 0:
            total[0], total[1] = out, dq
        else:
            total[0] += out
            total[1] += dq
        dv, dk = dot_nn(pb, grad), dot_nn(ds, query) * SCALE
        if i * STEP < BLOCK:
            gown[h, 0, rows, :] = dk
            gown[h, 1, rows, :] = dv
        else:
            there = pl.ds(i * STEP - BLOCK, STEP)
            gset[h, 0, there, :] = dk.astype(BF16)
            gset[h, 1, there, :] = dv.astype(BF16)
    lanes = pl.ds(pl.multiple_of(h * DIM, DIM), DIM)
    att[:, lanes] = total[0].T.astype(BF16)
    gq[:, lanes] = (total[1].T * SCALE).astype(BF16)


def kernel(
    q_hbm, k_hbm, v_hbm, g_hbm, att, gq, gk, gv,
    kv, q_all, g_all, pooled, told, heard, gown, gset, pair, csend, clow, cline, cin, csum, psend, pin, asend, ain,
    tsend, tin, hrecv, bias, mean, spread, score, dprob, total,
    send, recv, small_send, small_recv,
):
    g, s = lax.axis_index("grp"), lax.axis_index("seq")
    low, z = lax.div(g, 8), lax.rem(g, 8)
    high, x, core = lax.div(s, 8), lax.div(lax.rem(s, 8), 2), lax.rem(s, 2)
    other = 1 - core
    sibling = (g, s + 1 - 2 * core)
    slot_one = x * 4 + high * 2 + core
    across = ((1 - low) * 8 + z, s)
    has_prev = (g + s) > 0
    has_next = (g + s) < GROUPS + PLACES - 2
    up_group = lax.rem(g + lax.div(s + 1, PLACES), GROUPS)
    after = (up_group, lax.rem(s + 1, PLACES))
    low_group = lax.rem(g + GROUPS - 1 + lax.div(s + PLACES - 1, PLACES), GROUPS)
    before = (low_group, lax.rem(s + PLACES - 1, PLACES))

    def near_x(d):
        return lax.rem(x + d + 4, 4)

    def near_z(d):
        return lax.rem(z + d + 8, 8)

    def beside(d):
        return (g, high * 8 + near_x(d) * 2 + core)

    def along(d):
        return (low * 8 + near_z(d), s)

    def ranks(start, unit, count):
        return pl.ds(pl.multiple_of(start * unit, unit), count)

    def one_rows(column, row, count):
        return ranks(LEVEL1 // ONE + column * 4 + row * 2, ONE, count)

    def two_rows(group, count):
        return ranks(LEVEL2 // ONE + group, ONE, count)

    def loads(ch):
        return pl.ds(ch * PER_IN, PER_IN)

    def heads(ch):
        return pl.ds(ch * PER, PER)

    def lanes(h):
        return pl.ds(pl.multiple_of(h * DIM, DIM), DIM)

    def push(transfer, ch, src, dst, device):
        pltpu.make_async_remote_copy(
            src_ref=src, dst_ref=dst, send_sem=send.at[transfer, ch], recv_sem=recv.at[transfer, ch],
            device_id=device, device_id_type=MESH,
        ).start()

    def await_rows(sems, transfer, ch, rows):
        ref = kv.at[loads(ch) if transfer in FORWARD else heads(ch), 0, pl.ds(0, rows), :]
        pltpu.make_async_copy(ref, ref, sems.at[transfer, ch]).wait()

    def each_head(ch, do):
        lax.fori_loop(0, PER, lambda i, _: (do(ch * PER + i), 0)[1], 0)

    def fetch(h, _):
        ch = lax.div(h, PER_IN)
        for plane, src in enumerate((k_hbm, v_hbm)):
            pltpu.make_async_copy(
                src.at[:, lanes(h)], kv.at[h, plane, pl.ds(OWN, BLOCK), :], recv.at[IN_KV, ch]
            ).start()
        return 0

    def fetch_more(h, _):
        ch = lax.div(h, PER_IN)
        for dst, src in ((q_all, q_hbm), (g_all, g_hbm)):
            pltpu.make_async_copy(src.at[:, lanes(h)], dst.at[h], recv.at[IN_QG, ch]).start()
        return 0

    lax.fori_loop(0, HEADS, fetch, 0)
    lax.fori_loop(0, HEADS, fetch_more, 0)

    barrier = pltpu.get_barrier_semaphore()

    def meet(device):
        pl.semaphore_signal(barrier, inc=1, device_id=device, device_id_type=MESH)

    lax.fori_loop(1, PLACES, lambda j, _: (meet((g, lax.rem(s + j, PLACES))), 0)[1], 0)
    lax.fori_loop(1, 8, lambda d, _: (meet(along(d)), 0)[1], 0)
    meet(across)
    crosses_up = jnp.logical_and(s == PLACES - 1, has_next)
    crosses_down = jnp.logical_and(s == 0, has_prev)

    @pl.when(crosses_up)
    def _():
        pl.semaphore_signal(barrier, inc=1, device_id=after, device_id_type=MESH)

    @pl.when(crosses_down)
    def _():
        pl.semaphore_signal(barrier, inc=1, device_id=before, device_id_type=MESH)

    wide = (lax.broadcasted_iota(jnp.int32, (ONE, BLOCK), 0), lax.broadcasted_iota(jnp.int32, (ONE, BLOCK), 1))
    mean[...] = jnp.where(lax.shift_right_logical(wide[1], 4) == wide[0], 1.0 / POOL, 0.0).astype(BF16)
    tall = (lax.broadcasted_iota(jnp.int32, (BLOCK, ONE), 0), lax.broadcasted_iota(jnp.int32, (BLOCK, ONE), 1))
    spread[...] = jnp.where(lax.shift_right_logical(tall[0], 4) == tall[1], 1.0 / POOL, 0.0).astype(BF16)

    def pool_own(h, _):
        @pl.when(lax.rem(h, PER_IN) == 0)
        def _():
            await_rows(recv, IN_KV, lax.div(h, PER_IN), 2 * BLOCK)

        for plane in range(2):
            pooled[plane, h] = dot_nn(mean[...], kv[h, plane, pl.ds(OWN, BLOCK), :]).astype(BF16)
        kv[h, core, ranks(LEVEL1 // ONE + slot_one, ONE, ONE), :] = pooled[core, h]
        return 0

    lax.fori_loop(0, HEADS, pool_own, 0)
    told[...] = dot_nn(mean[...], pooled[...].reshape(2 * HEADS * ONE, DIM)).astype(BF16)
    heard[slot_one] = told[...]

    @pl.when(jnp.logical_not(has_prev))
    def _():
        kv[:, :, PREV:NEXT, :] = jnp.zeros((HEADS, 2, NEAR, DIM), BF16)
        hrecv[:, 0] = jnp.zeros((HEADS, 2, NEAR, DIM), BF16)

    @pl.when(jnp.logical_not(has_next))
    def _():
        kv[:, :, NEXT:LEVEL1, :] = jnp.zeros((HEADS, 2, NEAR, DIM), BF16)
        hrecv[:, 1] = jnp.zeros((HEADS, 2, NEAR, DIM), BF16)

    crosses = jnp.logical_or(crosses_up, crosses_down)

    @pl.when(crosses)
    def _():
        pl.semaphore_wait(barrier, PLACES - 1 + 8 + 1)

    @pl.when(jnp.logical_not(crosses))
    def _():
        pl.semaphore_wait(barrier, PLACES - 1 + 8)

    def tell(j, _):
        pltpu.make_async_remote_copy(
            src_ref=told, dst_ref=heard.at[slot_one],
            send_sem=small_send.at[0], recv_sem=small_recv.at[0],
            device_id=(g, lax.rem(s + j, PLACES)), device_id_type=MESH,
        ).start()
        return 0

    lax.fori_loop(1, PLACES, tell, 0)

    def await_small(sems, which, ref):
        pltpu.make_async_copy(ref, ref, sems.at[which]).wait()

    def spread_rows(v):
        upper = v.astype(BF16)
        rest = (v - upper.astype(F32)).astype(BF16)
        return dot_nn(spread[...], upper) + dot_nn(spread[...], rest)

    def tables():
        row = lax.broadcasted_iota(jnp.int32, (SET, DIM), 0)
        slot = lax.shift_right_logical(row & (BLOCK - 1), 5)
        place = (lax.shift_right_logical(slot, 1) & 1) * 8 + lax.shift_right_logical(slot, 2) * 2 + (slot & 1)
        dead_one = (row >= LEVEL1) & (row < LEVEL2) & (place >= s - 1) & (place <= s + 1)
        dead_two = (row >= LEVEL2) & (slot == g)
        no_prev = (row >= PREV) & (row < NEXT) & (g + s == 0)
        no_next = (row >= NEXT) & (row < LEVEL1) & (g + s == GROUPS + PLACES - 2)
        bias[...] = jnp.where(dead_one | dead_two | no_prev | no_next, FILL, 0.0)

    def own_coarse():
        await_small(small_recv, 0, heard.at[pl.ds(0, PLACES - 1)])
        shape = (HEADS * ONE, PLACES * ONE)
        to, come = lax.broadcasted_iota(jnp.int32, shape, 0), lax.broadcasted_iota(jnp.int32, shape, 1)
        head, within = lax.shift_right_logical(to, 5), to & 31
        wanted = lax.shift_right_logical(within, 1) * ONE + core * 16 + head * 2 + (within & 1)
        pick = jnp.where(come == wanted, 1.0, 0.0).astype(BF16)
        rows = dot_nn(pick, heard[...].reshape(PLACES * ONE, DIM)).astype(BF16)
        for h in range(HEADS):
            kv[h, core, two_rows(g, ONE), :] = rows[h * ONE : (h + 1) * ONE]

    def column(which):
        return (g, (1 - high) * 8 + x * 2 + which)

    def send_column(ch):
        hs = loads(ch)
        mine = ranks(LEVEL1 // ONE + slot_one, ONE, ONE)
        for plane in range(2):
            push(COLUMN, ch, pooled.at[plane, hs], kv.at[hs, plane, mine, :], column(plane))
        push(COLUMN, ch, pooled.at[other, hs], kv.at[hs, other, mine, :], sibling)

    def send_planes(ch):
        hs = loads(ch)
        await_rows(recv, COLUMN, ch, 3 * ONE)
        rows = kv.at[hs, core, one_rows(x, 0, 4 * ONE), :]
        for d in (2, 1, 3):
            push(BESIDE, ch, rows, rows, beside(d))

        @pl.when(ch == 0)
        def _():
            own_coarse()

        group = kv.at[hs, core, two_rows(g, ONE), :]
        for d in (4, 3, 5, 2, 6, 1, 7):
            push(ALONG, ch, group, group, along(d))

        @pl.when(has_next)
        def _():
            push(FROM_PREV, ch, kv.at[hs, :, pl.ds(OWN + BLOCK - NEAR, NEAR), :], kv.at[hs, :, pl.ds(PREV, NEAR), :], after)

        @pl.when(has_prev)
        def _():
            push(FROM_NEXT, ch, kv.at[hs, :, pl.ds(OWN, NEAR), :], kv.at[hs, :, pl.ds(NEXT, NEAR), :], before)

        @pl.when(ch == 0)
        def _():
            tables()

    def send_across(ch):
        hs = loads(ch)
        await_rows(recv, ALONG, ch, 7 * ONE)
        line = kv.at[hs, core, two_rows(low * 8, 8 * ONE), :]
        push(ACROSS, ch, line, line, across)

    def swap_set(ch):
        hs = loads(ch)
        await_rows(recv, BESIDE, ch, 12 * ONE)
        await_rows(recv, ACROSS, ch, 8 * ONE)
        whole = kv.at[hs, core, pl.ds(LEVEL1, 2 * BLOCK), :]
        push(PAIR_SET, ch, whole, whole, sibling)

    def await_set(ch):
        await_rows(recv, IN_QG, ch, 2 * BLOCK)
        await_rows(recv, PAIR_SET, ch, 2 * BLOCK)

        @pl.when(has_prev)
        def _():
            await_rows(recv, FROM_PREV, ch, 2 * NEAR)

        @pl.when(has_next)
        def _():
            await_rows(recv, FROM_NEXT, ch, 2 * NEAR)

    def compute(ch):
        hs = heads(ch)
        ready = lax.div(ch, PER_IN)
        pl.when(lax.rem(ch, PER_IN) == 0)(functools.partial(await_set, ready))
        each_head(
            ch,
            lambda h: attend(h, q_all, g_all, kv, bias, att, gq, gown, gset, score, dprob, total),
        )
        push(PAIR_GRAD, ch, gset.at[hs, other, pl.ds(LEVEL1 - BLOCK, 2 * BLOCK), :], pair.at[hs], sibling)

        @pl.when(has_prev)
        def _():
            push(GRAD_NEXT, ch, gset.at[hs, :, pl.ds(PREV - BLOCK, NEAR), :], hrecv.at[hs, 1], before)

        @pl.when(has_next)
        def _():
            push(GRAD_PREV, ch, gset.at[hs, :, pl.ds(NEXT - BLOCK, NEAR), :], hrecv.at[hs, 0], after)

    def added(a, b):
        return (a.astype(F32) + b.astype(F32)).astype(BF16)

    def send_grads(ch):
        hs = heads(ch)
        await_rows(recv, PAIR_GRAD, ch, 2 * BLOCK)

        def add(h):
            psend[h] = added(gset[h, core, pl.ds(LEVEL1 - BLOCK, BLOCK), :], pair[h, pl.ds(0, BLOCK), :])
            csend[h] = added(gset[h, core, pl.ds(LEVEL2 - BLOCK, BLOCK), :], pair[h, pl.ds(BLOCK, BLOCK), :])

        each_head(ch, add)
        for d in (2, 1, 3):
            push(
                BESIDE_GRAD, ch, psend.at[hs, ranks(near_x(d), 128, 128), :],
                pin.at[hs, ranks(x, 128, 128), :], beside(d),
            )
        push(
            ACROSS_GRAD, ch, csend.at[hs, ranks((1 - low) * 8, ONE, 8 * ONE), :], clow.at[hs], across,
        )

    def column_grads(ch):
        hs = heads(ch)
        await_rows(recv, BESIDE_GRAD, ch, 12 * ONE)

        def add(h):
            v = psend[h, ranks(x, 128, 128), :].astype(F32)
            for d in range(1, 4):
                v = v + pin[h, ranks(near_x(d), 128, 128), :].astype(F32)
            asend[h] = v.astype(BF16)
            ain[h, ranks(core * 2 + high, ONE, ONE), :] = asend[h, ranks(high * 2 + core, ONE, ONE), :]

        each_head(ch, add)
        place = ain.at[hs, ranks(core * 2 + high, ONE, ONE), :]
        for which in range(2):
            push(
                COLUMN_GRAD, ch, asend.at[hs, ranks((1 - high) * 2 + which, ONE, ONE), :], place,
                column(which),
            )
        push(COLUMN_GRAD, ch, asend.at[hs, ranks(high * 2 + other, ONE, ONE), :], place, sibling)
        await_rows(recv, ACROSS_GRAD, ch, 8 * ONE)

        def add_line(h):
            cline[h] = added(csend[h, ranks(low * 8, ONE, 8 * ONE), :], clow[h])

        each_head(ch, add_line)
        for d in (4, 3, 5, 2, 6, 1, 7):
            push(
                ALONG_GRAD, ch, cline.at[hs, ranks(near_z(d), ONE, ONE), :],
                cin.at[hs, ranks(z, ONE, ONE), :], along(d),
            )

    def coarse_sums(ch):
        await_rows(recv, ALONG_GRAD, ch, 7 * ONE)

        def add(h):
            v = cline[h, ranks(z, ONE, ONE), :].astype(F32)
            for d in range(1, 8):
                v = v + cin[h, ranks(near_z(d), ONE, ONE), :].astype(F32)
            csum[h] = v.astype(BF16)

        each_head(ch, add)

    def finish(ch):
        await_rows(recv, COLUMN_GRAD, ch, 3 * ONE)

        @pl.when(has_prev)
        def _():
            await_rows(recv, GRAD_PREV, ch, 2 * NEAR)

        @pl.when(has_next)
        def _():
            await_rows(recv, GRAD_NEXT, ch, 2 * NEAR)

        def add(h):
            for plane in range(2):
                level = ain[h, pl.ds(2 * plane * ONE, ONE), :].astype(F32)
                level = level + ain[h, pl.ds((2 * plane + 1) * ONE, ONE), :].astype(F32)
                sums = gown[h, plane] + spread_rows(level)
                for side in range(2):
                    rows = slice(side * NEAR, (side + 1) * NEAR)
                    gown[h, plane, rows, :] = sums[rows] + hrecv[h, side, plane].astype(F32)

        each_head(ch, add)

    inward = (send_column, send_planes, send_across, swap_set)
    outward = (compute, send_grads, column_grads, coarse_sums, finish)
    lead = len(inward) - 1

    def step(t, _):
        pl.when(jnp.logical_and(t >= lead + 1, t < CHUNKS + lead + 1))(lambda: compute(t - lead - 1))
        for i, stage in enumerate(outward[1:]):
            lag = lead + 2 + i
            pl.when(jnp.logical_and(t >= lag, t < CHUNKS + lag))(functools.partial(stage, t - lag))
            if stage is coarse_sums:
                pl.when(t == CHUNKS + lag - 1)(send_coarse_sums)
        for lag, stage in enumerate(inward):
            first, last = 2 * (t - lag) - 1, 2 * (t - lag) + 1
            lax.fori_loop(
                jnp.maximum(first, 0), jnp.minimum(last, LOADS), lambda ch, _: (stage(ch), 0)[1], 0
            )
        return 0

    def send_coarse_sums():
        shape = (HEADS * ONE, HEADS * ONE)
        to, come = lax.broadcasted_iota(jnp.int32, shape, 0), lax.broadcasted_iota(jnp.int32, shape, 1)
        target, within = lax.shift_right_logical(to, 4), to & 15
        wanted = lax.shift_right_logical(within, 1) * ONE + target * 2 + (within & 1)
        pick = jnp.where(come == wanted, 1.0, 0.0).astype(BF16)
        tsend[...] = dot_nn(pick, csum[...].reshape(HEADS * ONE, DIM)).astype(BF16)
        source = high * 4 + x
        tin[core, source] = tsend[ranks(slot_one, 16, 16), :]

        def tell_sums(j, _):
            place = lax.rem(s + j, PLACES)
            slot = lax.div(lax.rem(place, 8), 2) * 4 + lax.div(place, 8) * 2 + lax.rem(place, 2)
            pltpu.make_async_remote_copy(
                src_ref=tsend.at[ranks(slot, 16, 16), :], dst_ref=tin.at[core, source],
                send_sem=small_send.at[1], recv_sem=small_recv.at[1],
                device_id=(g, place), device_id_type=MESH,
            ).start()
            return 0

        lax.fori_loop(1, PLACES, tell_sums, 0)

    lax.fori_loop(0, CHUNKS + lead + len(outward), step, 0)

    sums_in = tsend.at[pl.ds(0, (PLACES - 1) * 16), :]
    await_small(small_recv, 1, sums_in)
    for plane, dst in enumerate((gk, gv)):
        coarse = tin[plane, 0].astype(F32)
        for i in range(1, 8):
            coarse = coarse + tin[plane, i].astype(F32)
        coarse = coarse * (1.0 / (POOL * POOL))
        for h in range(HEADS):
            for side in range(2):
                rows = slice(side * NEAR, (side + 1) * NEAR)
                row = coarse[2 * h + side : 2 * h + side + 1]
                dst[rows, h * DIM : (h + 1) * DIM] = (gown[h, plane, rows, :] + row).astype(BF16)

    await_small(small_send, 0, heard.at[pl.ds(0, PLACES - 1)])
    await_small(small_send, 1, sums_in)

    def drain(ch, _):
        for transfer, rows in (
            (PAIR_GRAD, 1024), (ACROSS_GRAD, 256), (ALONG_GRAD, 224), (BESIDE_GRAD, 384), (COLUMN_GRAD, 96),
        ):
            await_rows(send, transfer, ch, rows)
        pl.when(has_prev)(lambda: await_rows(send, GRAD_NEXT, ch, 2 * NEAR))
        pl.when(has_next)(lambda: await_rows(send, GRAD_PREV, ch, 2 * NEAR))
        return 0

    def drain_in(ch, _):
        for transfer, rows in ((COLUMN, 96), (BESIDE, 384), (ALONG, 224), (ACROSS, 256), (PAIR_SET, 1024)):
            await_rows(send, transfer, ch, rows)
        pl.when(has_prev)(lambda: await_rows(send, FROM_NEXT, ch, 2 * NEAR))
        pl.when(has_next)(lambda: await_rows(send, FROM_PREV, ch, 2 * NEAR))
        return 0

    lax.fori_loop(0, LOADS, drain_in, 0)
    lax.fori_loop(0, CHUNKS, drain, 0)


def body(query_rows, key_rows, value_rows, grad_out):
    shape = pltpu.VMEM(query_rows.shape, BF16)

    def rows(count, *lead):
        return ((*lead, HEADS, count, DIM), BF16)

    scratch = [
        ((HEADS, 2, SET, DIM), BF16),
        rows(BLOCK),
        rows(BLOCK),
        rows(ONE, 2),
        ((ONE, DIM), BF16),
        ((PLACES, ONE, DIM), BF16),
        ((HEADS, 2, BLOCK, DIM), F32),
        ((HEADS, 2, SET - BLOCK, DIM), BF16),
        rows(2 * BLOCK),
        rows(BLOCK),
        rows(8 * ONE),
        rows(8 * ONE),
        rows(8 * ONE),
        rows(ONE),
        rows(BLOCK),
        rows(BLOCK),
        rows(128),
        rows(128),
        ((HEADS * ONE, DIM), BF16),
        ((2, 8, 16, DIM), BF16),
        ((HEADS, 2, 2, NEAR, DIM), BF16),
        ((SET, DIM), F32),
        ((ONE, BLOCK), BF16),
        ((BLOCK, ONE), BF16),
        ((SET, BLOCK), F32),
        ((SET, BLOCK), F32),
        ((2, DIM, BLOCK), F32),
    ]
    anywhere = pl.BlockSpec(memory_space=pl.ANY)
    return pl.pallas_call(
        kernel,
        out_shape=[shape] * 4,
        in_specs=[anywhere] * 4,
        out_specs=[pl.BlockSpec(memory_space=pltpu.VMEM)] * 4,
        scratch_shapes=[pltpu.VMEM(*one) for one in scratch]
        + [pltpu.SemaphoreType.DMA((TRANSFERS, CHUNKS))] * 2
        + [pltpu.SemaphoreType.DMA((2,))] * 2,
        compiler_params=pltpu.CompilerParams(
            collective_id=0, has_side_effects=True, vmem_limit_bytes=50 << 20
        ),
        name="hierarchical",
    )(query_rows, key_rows, value_rows, grad_out)


def solution(mesh):
    placed = P(("grp", "seq"), None)
    return jax.shard_map(
        body, mesh=mesh, in_specs=(placed,) * 4, out_specs=(placed,) * 4, check_vma=False
    )
```

```python
import functools

import jax
import jax.numpy as jnp
from jax import lax
from jax.experimental import pallas as pl
from jax.experimental.pallas import tpu as pltpu
from jax.sharding import PartitionSpec as P

F32 = jnp.float32
BF16 = jnp.bfloat16
HEADS = 8
DIM = 128
BLOCK = 512
NEAR = 256
POOL = 16
ONE = BLOCK // POOL
TWO = ONE // POOL
PLACES = 16
GROUPS = 16
SET = 2048
OWN, PREV, NEXT, LEVEL1, LEVEL2 = 0, 512, 768, 1024, 1536
SCALE = DIM**-0.5
SCALE2 = SCALE * 1.4426950408889634
FILL = -1e30
MESH = pl.DeviceIdType.MESH
CHUNKS = 8
PER = 1
STEP = 512

IN_KV, IN_QG, COLUMN, BESIDE, ALONG, ACROSS, PAIR_SET, FROM_PREV = range(0, 8)
FROM_NEXT, PAIR_GRAD, GRAD_PREV, GRAD_NEXT, ALONG_GRAD, ACROSS_GRAD, BESIDE_GRAD, COLUMN_GRAD = range(8, 16)
TRANSFERS = 16
FORWARD = (IN_KV, IN_QG, COLUMN, BESIDE, ALONG, ACROSS, PAIR_SET, FROM_PREV, FROM_NEXT)
PER_IN = 1
LOADS = HEADS // PER_IN


def dot_nt(a, b):
    return lax.dot_general(a, b, (((1,), (1,)), ((), ())), preferred_element_type=F32)


def dot_tn(a, b):
    return lax.dot_general(a, b, (((0,), (0,)), ((), ())), preferred_element_type=F32)


def dot_nn(a, b):
    return jnp.dot(a, b, preferred_element_type=F32)


def attend(h, q_all, g_all, kv, bias, att, gq, gown, gset, score, dprob, total):
    query, grad = q_all[h], g_all[h]
    parts = [pl.ds(i * STEP, STEP) for i in range(SET // STEP)]

    def folded(x, op):
        return op(x.reshape(STEP // 8, 8, BLOCK), axis=0)

    top = None
    for rows in parts:
        s = dot_nt(kv[h, 0, rows, :], query)
        b = bias[rows, :]
        s = s + jnp.concatenate([b] * (BLOCK // DIM), axis=1)
        score[rows, :] = s
        part = folded(s, jnp.max)
        top = part if top is None else jnp.maximum(top, part)
    top = jnp.max(top, axis=0, keepdims=True)
    norm = mixed = None
    for rows in parts:
        dp = dot_nt(kv[h, 1, rows, :], grad)
        e = jnp.exp2((score[rows, :] - top) * SCALE2)
        score[rows, :] = e
        dprob[rows, :] = dp
        part, other = folded(e, jnp.sum), folded(e * dp, jnp.sum)
        norm = part if norm is None else norm + part
        mixed = other if mixed is None else mixed + other
    inverse = 1.0 / jnp.sum(norm, axis=0, keepdims=True)
    delta = jnp.sum(mixed, axis=0, keepdims=True) * inverse
    for i, rows in enumerate(parts):
        p = score[rows, :] * inverse
        pb = p.astype(BF16)
        ds = (p * (dprob[rows, :] - delta)).astype(BF16)
        out, dq = dot_tn(kv[h, 1, rows, :], pb), dot_tn(kv[h, 0, rows, :], ds)
        if i == 0:
            total[0], total[1] = out, dq
        else:
            total[0] += out
            total[1] += dq
        dv, dk = dot_nn(pb, grad), dot_nn(ds, query) * SCALE
        if i * STEP < BLOCK:
            gown[h, 0, rows, :] = dk
            gown[h, 1, rows, :] = dv
        else:
            there = pl.ds(i * STEP - BLOCK, STEP)
            gset[h, 0, there, :] = dk.astype(BF16)
            gset[h, 1, there, :] = dv.astype(BF16)
    lanes = pl.ds(pl.multiple_of(h * DIM, DIM), DIM)
    att[:, lanes] = total[0].T.astype(BF16)
    gq[:, lanes] = (total[1].T * SCALE).astype(BF16)


def kernel(
    q_hbm, k_hbm, v_hbm, g_hbm, att, gq, gk, gv,
    kv, q_all, g_all, pooled, told, heard, gown, gset, pair, csend, clow, cline, cin, csum, psend, pin, asend, ain,
    tsend, tin, hrecv, bias, mean, spread, score, dprob, total,
    send, recv, small_send, small_recv,
):
    g, s = lax.axis_index("grp"), lax.axis_index("seq")
    low, z = lax.div(g, 8), lax.rem(g, 8)
    high, x, core = lax.div(s, 8), lax.div(lax.rem(s, 8), 2), lax.rem(s, 2)
    other = 1 - core
    sibling = (g, s + 1 - 2 * core)
    slot_one = x * 4 + high * 2 + core
    across = ((1 - low) * 8 + z, s)
    has_prev = (g + s) > 0
    has_next = (g + s) < GROUPS + PLACES - 2
    up_group = lax.rem(g + lax.div(s + 1, PLACES), GROUPS)
    after = (up_group, lax.rem(s + 1, PLACES))
    low_group = lax.rem(g + GROUPS - 1 + lax.div(s + PLACES - 1, PLACES), GROUPS)
    before = (low_group, lax.rem(s + PLACES - 1, PLACES))

    def near_x(d):
        return lax.rem(x + d + 4, 4)

    def near_z(d):
        return lax.rem(z + d + 8, 8)

    def beside(d):
        return (g, high * 8 + near_x(d) * 2 + core)

    def along(d):
        return (low * 8 + near_z(d), s)

    def ranks(start, unit, count):
        return pl.ds(pl.multiple_of(start * unit, unit), count)

    def one_rows(column, row, count):
        return ranks(LEVEL1 // ONE + column * 4 + row * 2, ONE, count)

    def two_rows(group, count):
        return ranks(LEVEL2 // ONE + group, ONE, count)

    def loads(ch):
        return pl.ds(ch * PER_IN, PER_IN)

    def heads(ch):
        return pl.ds(ch * PER, PER)

    def lanes(h):
        return pl.ds(pl.multiple_of(h * DIM, DIM), DIM)

    def push(transfer, ch, src, dst, device):
        pltpu.make_async_remote_copy(
            src_ref=src, dst_ref=dst, send_sem=send.at[transfer, ch], recv_sem=recv.at[transfer, ch],
            device_id=device, device_id_type=MESH,
        ).start()

    def await_rows(sems, transfer, ch, rows):
        ref = kv.at[loads(ch) if transfer in FORWARD else heads(ch), 0, pl.ds(0, rows), :]
        pltpu.make_async_copy(ref, ref, sems.at[transfer, ch]).wait()

    def each_head(ch, do):
        lax.fori_loop(0, PER, lambda i, _: (do(ch * PER + i), 0)[1], 0)

    def fetch(h, _):
        ch = lax.div(h, PER_IN)
        for plane, src in enumerate((k_hbm, v_hbm)):
            pltpu.make_async_copy(
                src.at[:, lanes(h)], kv.at[h, plane, pl.ds(OWN, BLOCK), :], recv.at[IN_KV, ch]
            ).start()
        return 0

    def fetch_more(h, _):
        ch = lax.div(h, PER_IN)
        for dst, src in ((q_all, q_hbm), (g_all, g_hbm)):
            pltpu.make_async_copy(src.at[:, lanes(h)], dst.at[h], recv.at[IN_QG, ch]).start()
        return 0

    lax.fori_loop(0, HEADS, fetch, 0)
    lax.fori_loop(0, HEADS, fetch_more, 0)

    barrier = pltpu.get_barrier_semaphore()

    def meet(device):
        pl.semaphore_signal(barrier, inc=1, device_id=device, device_id_type=MESH)

    lax.fori_loop(1, PLACES, lambda j, _: (meet((g, lax.rem(s + j, PLACES))), 0)[1], 0)
    lax.fori_loop(1, 8, lambda d, _: (meet(along(d)), 0)[1], 0)
    meet(across)
    crosses_up = jnp.logical_and(s == PLACES - 1, has_next)
    crosses_down = jnp.logical_and(s == 0, has_prev)

    @pl.when(crosses_up)
    def _():
        pl.semaphore_signal(barrier, inc=1, device_id=after, device_id_type=MESH)

    @pl.when(crosses_down)
    def _():
        pl.semaphore_signal(barrier, inc=1, device_id=before, device_id_type=MESH)

    wide = (lax.broadcasted_iota(jnp.int32, (ONE, BLOCK), 0), lax.broadcasted_iota(jnp.int32, (ONE, BLOCK), 1))
    mean[...] = jnp.where(lax.shift_right_logical(wide[1], 4) == wide[0], 1.0 / POOL, 0.0).astype(BF16)
    tall = (lax.broadcasted_iota(jnp.int32, (BLOCK, ONE), 0), lax.broadcasted_iota(jnp.int32, (BLOCK, ONE), 1))
    spread[...] = jnp.where(lax.shift_right_logical(tall[0], 4) == tall[1], 1.0 / POOL, 0.0).astype(BF16)

    def pool_own(h, _):
        @pl.when(lax.rem(h, PER_IN) == 0)
        def _():
            await_rows(recv, IN_KV, lax.div(h, PER_IN), 2 * BLOCK)

        for plane in range(2):
            pooled[plane, h] = dot_nn(mean[...], kv[h, plane, pl.ds(OWN, BLOCK), :]).astype(BF16)
        kv[h, core, ranks(LEVEL1 // ONE + slot_one, ONE, ONE), :] = pooled[core, h]
        return 0

    lax.fori_loop(0, HEADS, pool_own, 0)
    told[...] = dot_nn(mean[...], pooled[...].reshape(2 * HEADS * ONE, DIM)).astype(BF16)
    heard[slot_one] = told[...]

    @pl.when(jnp.logical_not(has_prev))
    def _():
        kv[:, :, PREV:NEXT, :] = jnp.zeros((HEADS, 2, NEAR, DIM), BF16)
        hrecv[:, 0] = jnp.zeros((HEADS, 2, NEAR, DIM), BF16)

    @pl.when(jnp.logical_not(has_next))
    def _():
        kv[:, :, NEXT:LEVEL1, :] = jnp.zeros((HEADS, 2, NEAR, DIM), BF16)
        hrecv[:, 1] = jnp.zeros((HEADS, 2, NEAR, DIM), BF16)

    crosses = jnp.logical_or(crosses_up, crosses_down)

    @pl.when(crosses)
    def _():
        pl.semaphore_wait(barrier, PLACES - 1 + 8 + 1)

    @pl.when(jnp.logical_not(crosses))
    def _():
        pl.semaphore_wait(barrier, PLACES - 1 + 8)

    def tell(j, _):
        pltpu.make_async_remote_copy(
            src_ref=told, dst_ref=heard.at[slot_one],
            send_sem=small_send.at[0], recv_sem=small_recv.at[0],
            device_id=(g, lax.rem(s + j, PLACES)), device_id_type=MESH,
        ).start()
        return 0

    lax.fori_loop(1, PLACES, tell, 0)

    def await_small(sems, which, ref):
        pltpu.make_async_copy(ref, ref, sems.at[which]).wait()

    def spread_rows(v):
        upper = v.astype(BF16)
        rest = (v - upper.astype(F32)).astype(BF16)
        return dot_nn(spread[...], upper) + dot_nn(spread[...], rest)

    def tables():
        row = lax.broadcasted_iota(jnp.int32, (SET, DIM), 0)
        slot = lax.shift_right_logical(row & (BLOCK - 1), 5)
        place = (lax.shift_right_logical(slot, 1) & 1) * 8 + lax.shift_right_logical(slot, 2) * 2 + (slot & 1)
        dead_one = (row >= LEVEL1) & (row < LEVEL2) & (place >= s - 1) & (place <= s + 1)
        dead_two = (row >= LEVEL2) & (slot == g)
        no_prev = (row >= PREV) & (row < NEXT) & (g + s == 0)
        no_next = (row >= NEXT) & (row < LEVEL1) & (g + s == GROUPS + PLACES - 2)
        bias[...] = jnp.where(dead_one | dead_two | no_prev | no_next, FILL, 0.0)

    def own_coarse():
        await_small(small_recv, 0, heard.at[pl.ds(0, PLACES - 1)])
        shape = (HEADS * ONE, PLACES * ONE)
        to, come = lax.broadcasted_iota(jnp.int32, shape, 0), lax.broadcasted_iota(jnp.int32, shape, 1)
        head, within = lax.shift_right_logical(to, 5), to & 31
        wanted = lax.shift_right_logical(within, 1) * ONE + core * 16 + head * 2 + (within & 1)
        pick = jnp.where(come == wanted, 1.0, 0.0).astype(BF16)
        rows = dot_nn(pick, heard[...].reshape(PLACES * ONE, DIM)).astype(BF16)
        for h in range(HEADS):
            kv[h, core, two_rows(g, ONE), :] = rows[h * ONE : (h + 1) * ONE]

    def column(which):
        return (g, (1 - high) * 8 + x * 2 + which)

    def send_column(ch):
        hs = loads(ch)
        mine = ranks(LEVEL1 // ONE + slot_one, ONE, ONE)
        for plane in range(2):
            push(COLUMN, ch, pooled.at[plane, hs], kv.at[hs, plane, mine, :], column(plane))
        push(COLUMN, ch, pooled.at[other, hs], kv.at[hs, other, mine, :], sibling)

        @pl.when(has_next)
        def _():
            push(FROM_PREV, ch, kv.at[hs, :, pl.ds(OWN + BLOCK - NEAR, NEAR), :], kv.at[hs, :, pl.ds(PREV, NEAR), :], after)

        @pl.when(has_prev)
        def _():
            push(FROM_NEXT, ch, kv.at[hs, :, pl.ds(OWN, NEAR), :], kv.at[hs, :, pl.ds(NEXT, NEAR), :], before)

    def send_planes(ch):
        hs = loads(ch)
        await_rows(recv, COLUMN, ch, 3 * ONE)
        rows = kv.at[hs, core, one_rows(x, 0, 4 * ONE), :]
        for d in (2, 1, 3):
            push(BESIDE, ch, rows, rows, beside(d))

        @pl.when(ch == 0)
        def _():
            own_coarse()

        group = kv.at[hs, core, two_rows(g, ONE), :]
        for d in (4, 3, 5, 2, 6, 1, 7):
            push(ALONG, ch, group, group, along(d))

        @pl.when(ch == 0)
        def _():
            tables()

    def send_across(ch):
        hs = loads(ch)
        await_rows(recv, ALONG, ch, 7 * ONE)
        line = kv.at[hs, core, two_rows(low * 8, 8 * ONE), :]
        push(ACROSS, ch, line, line, across)

    def swap_set(ch):
        hs = loads(ch)
        await_rows(recv, BESIDE, ch, 12 * ONE)
        await_rows(recv, ACROSS, ch, 8 * ONE)
        whole = kv.at[hs, core, pl.ds(LEVEL1, 2 * BLOCK), :]
        push(PAIR_SET, ch, whole, whole, sibling)

    def await_set(ch):
        await_rows(recv, IN_QG, ch, 2 * BLOCK)
        await_rows(recv, PAIR_SET, ch, 2 * BLOCK)

        @pl.when(has_prev)
        def _():
            await_rows(recv, FROM_PREV, ch, 2 * NEAR)

        @pl.when(has_next)
        def _():
            await_rows(recv, FROM_NEXT, ch, 2 * NEAR)

    def compute(ch):
        hs = heads(ch)
        ready = lax.div(ch, PER_IN)
        pl.when(lax.rem(ch, PER_IN) == 0)(functools.partial(await_set, ready))
        each_head(
            ch,
            lambda h: attend(h, q_all, g_all, kv, bias, att, gq, gown, gset, score, dprob, total),
        )
        push(PAIR_GRAD, ch, gset.at[hs, other, pl.ds(LEVEL1 - BLOCK, 2 * BLOCK), :], pair.at[hs], sibling)

        @pl.when(has_prev)
        def _():
            push(GRAD_NEXT, ch, gset.at[hs, :, pl.ds(PREV - BLOCK, NEAR), :], hrecv.at[hs, 1], before)

        @pl.when(has_next)
        def _():
            push(GRAD_PREV, ch, gset.at[hs, :, pl.ds(NEXT - BLOCK, NEAR), :], hrecv.at[hs, 0], after)

    def added(a, b):
        return (a.astype(F32) + b.astype(F32)).astype(BF16)

    def send_grads(ch):
        hs = heads(ch)
        await_rows(recv, PAIR_GRAD, ch, 2 * BLOCK)

        def add(h):
            psend[h] = added(gset[h, core, pl.ds(LEVEL1 - BLOCK, BLOCK), :], pair[h, pl.ds(0, BLOCK), :])
            csend[h] = added(gset[h, core, pl.ds(LEVEL2 - BLOCK, BLOCK), :], pair[h, pl.ds(BLOCK, BLOCK), :])

        each_head(ch, add)
        for d in (2, 1, 3):
            push(
                BESIDE_GRAD, ch, psend.at[hs, ranks(near_x(d), 128, 128), :],
                pin.at[hs, ranks(x, 128, 128), :], beside(d),
            )
        push(
            ACROSS_GRAD, ch, csend.at[hs, ranks((1 - low) * 8, ONE, 8 * ONE), :], clow.at[hs], across,
        )

    def column_grads(ch):
        hs = heads(ch)
        await_rows(recv, BESIDE_GRAD, ch, 12 * ONE)

        def add(h):
            v = psend[h, ranks(x, 128, 128), :].astype(F32)
            for d in range(1, 4):
                v = v + pin[h, ranks(near_x(d), 128, 128), :].astype(F32)
            asend[h] = v.astype(BF16)
            ain[h, ranks(core * 2 + high, ONE, ONE), :] = asend[h, ranks(high * 2 + core, ONE, ONE), :]

        each_head(ch, add)
        place = ain.at[hs, ranks(core * 2 + high, ONE, ONE), :]
        for which in range(2):
            push(
                COLUMN_GRAD, ch, asend.at[hs, ranks((1 - high) * 2 + which, ONE, ONE), :], place,
                column(which),
            )
        push(COLUMN_GRAD, ch, asend.at[hs, ranks(high * 2 + other, ONE, ONE), :], place, sibling)
        await_rows(recv, ACROSS_GRAD, ch, 8 * ONE)

        def add_line(h):
            cline[h] = added(csend[h, ranks(low * 8, ONE, 8 * ONE), :], clow[h])

        each_head(ch, add_line)
        for d in (4, 3, 5, 2, 6, 1, 7):
            push(
                ALONG_GRAD, ch, cline.at[hs, ranks(near_z(d), ONE, ONE), :],
                cin.at[hs, ranks(z, ONE, ONE), :], along(d),
            )

    def coarse_sums(ch):
        await_rows(recv, ALONG_GRAD, ch, 7 * ONE)

        def add(h):
            v = cline[h, ranks(z, ONE, ONE), :].astype(F32)
            for d in range(1, 8):
                v = v + cin[h, ranks(near_z(d), ONE, ONE), :].astype(F32)
            csum[h] = v.astype(BF16)

        each_head(ch, add)

    def finish(ch):
        await_rows(recv, COLUMN_GRAD, ch, 3 * ONE)

        @pl.when(has_prev)
        def _():
            await_rows(recv, GRAD_PREV, ch, 2 * NEAR)

        @pl.when(has_next)
        def _():
            await_rows(recv, GRAD_NEXT, ch, 2 * NEAR)

        def add(h):
            for plane in range(2):
                level = ain[h, pl.ds(2 * plane * ONE, ONE), :].astype(F32)
                level = level + ain[h, pl.ds((2 * plane + 1) * ONE, ONE), :].astype(F32)
                sums = gown[h, plane] + spread_rows(level)
                for side in range(2):
                    rows = slice(side * NEAR, (side + 1) * NEAR)
                    gown[h, plane, rows, :] = sums[rows] + hrecv[h, side, plane].astype(F32)

        each_head(ch, add)

    inward = (send_column, send_planes, send_across, swap_set)
    outward = (compute, send_grads, column_grads, coarse_sums, finish)
    lead = len(inward) - 1

    def step(t, _):
        pl.when(jnp.logical_and(t >= lead + 1, t < CHUNKS + lead + 1))(lambda: compute(t - lead - 1))
        for i, stage in enumerate(outward[1:]):
            lag = lead + 2 + i
            pl.when(jnp.logical_and(t >= lag, t < CHUNKS + lag))(functools.partial(stage, t - lag))
            if stage is coarse_sums:
                pl.when(t == CHUNKS + lag - 1)(send_coarse_sums)
        for lag, stage in enumerate(inward):
            first, last = 2 * (t - lag) - 1, 2 * (t - lag) + 1
            lax.fori_loop(
                jnp.maximum(first, 0), jnp.minimum(last, LOADS), lambda ch, _: (stage(ch), 0)[1], 0
            )
        return 0

    def send_coarse_sums():
        shape = (HEADS * ONE, HEADS * ONE)
        to, come = lax.broadcasted_iota(jnp.int32, shape, 0), lax.broadcasted_iota(jnp.int32, shape, 1)
        target, within = lax.shift_right_logical(to, 4), to & 15
        wanted = lax.shift_right_logical(within, 1) * ONE + target * 2 + (within & 1)
        pick = jnp.where(come == wanted, 1.0, 0.0).astype(BF16)
        tsend[...] = dot_nn(pick, csum[...].reshape(HEADS * ONE, DIM)).astype(BF16)
        source = high * 4 + x
        tin[core, source] = tsend[ranks(slot_one, 16, 16), :]

        def tell_sums(j, _):
            place = lax.rem(s + j, PLACES)
            slot = lax.div(lax.rem(place, 8), 2) * 4 + lax.div(place, 8) * 2 + lax.rem(place, 2)
            pltpu.make_async_remote_copy(
                src_ref=tsend.at[ranks(slot, 16, 16), :], dst_ref=tin.at[core, source],
                send_sem=small_send.at[1], recv_sem=small_recv.at[1],
                device_id=(g, place), device_id_type=MESH,
            ).start()
            return 0

        lax.fori_loop(1, PLACES, tell_sums, 0)

    lax.fori_loop(0, CHUNKS + lead + len(outward), step, 0)

    sums_in = tsend.at[pl.ds(0, (PLACES - 1) * 16), :]
    await_small(small_recv, 1, sums_in)
    for plane, dst in enumerate((gk, gv)):
        coarse = tin[plane, 0].astype(F32)
        for i in range(1, 8):
            coarse = coarse + tin[plane, i].astype(F32)
        coarse = coarse * (1.0 / (POOL * POOL))
        for h in range(HEADS):
            for side in range(2):
                rows = slice(side * NEAR, (side + 1) * NEAR)
                row = coarse[2 * h + side : 2 * h + side + 1]
                dst[rows, h * DIM : (h + 1) * DIM] = (gown[h, plane, rows, :] + row).astype(BF16)

    await_small(small_send, 0, heard.at[pl.ds(0, PLACES - 1)])
    await_small(small_send, 1, sums_in)

    def drain(ch, _):
        for transfer, rows in (
            (PAIR_GRAD, 1024), (ACROSS_GRAD, 256), (ALONG_GRAD, 224), (BESIDE_GRAD, 384), (COLUMN_GRAD, 96),
        ):
            await_rows(send, transfer, ch, rows)
        pl.when(has_prev)(lambda: await_rows(send, GRAD_NEXT, ch, 2 * NEAR))
        pl.when(has_next)(lambda: await_rows(send, GRAD_PREV, ch, 2 * NEAR))
        return 0

    def drain_in(ch, _):
        for transfer, rows in ((COLUMN, 96), (BESIDE, 384), (ALONG, 224), (ACROSS, 256), (PAIR_SET, 1024)):
            await_rows(send, transfer, ch, rows)
        pl.when(has_prev)(lambda: await_rows(send, FROM_NEXT, ch, 2 * NEAR))
        pl.when(has_next)(lambda: await_rows(send, FROM_PREV, ch, 2 * NEAR))
        return 0

    lax.fori_loop(0, LOADS, drain_in, 0)
    lax.fori_loop(0, CHUNKS, drain, 0)


def body(query_rows, key_rows, value_rows, grad_out):
    shape = pltpu.VMEM(query_rows.shape, BF16)

    def rows(count, *lead):
        return ((*lead, HEADS, count, DIM), BF16)

    scratch = [
        ((HEADS, 2, SET, DIM), BF16),
        rows(BLOCK),
        rows(BLOCK),
        rows(ONE, 2),
        ((ONE, DIM), BF16),
        ((PLACES, ONE, DIM), BF16),
        ((HEADS, 2, BLOCK, DIM), F32),
        ((HEADS, 2, SET - BLOCK, DIM), BF16),
        rows(2 * BLOCK),
        rows(BLOCK),
        rows(8 * ONE),
        rows(8 * ONE),
        rows(8 * ONE),
        rows(ONE),
        rows(BLOCK),
        rows(BLOCK),
        rows(128),
        rows(128),
        ((HEADS * ONE, DIM), BF16),
        ((2, 8, 16, DIM), BF16),
        ((HEADS, 2, 2, NEAR, DIM), BF16),
        ((SET, DIM), F32),
        ((ONE, BLOCK), BF16),
        ((BLOCK, ONE), BF16),
        ((SET, BLOCK), F32),
        ((SET, BLOCK), F32),
        ((2, DIM, BLOCK), F32),
    ]
    anywhere = pl.BlockSpec(memory_space=pl.ANY)
    return pl.pallas_call(
        kernel,
        out_shape=[shape] * 4,
        in_specs=[anywhere] * 4,
        out_specs=[pl.BlockSpec(memory_space=pltpu.VMEM)] * 4,
        scratch_shapes=[pltpu.VMEM(*one) for one in scratch]
        + [pltpu.SemaphoreType.DMA((TRANSFERS, CHUNKS))] * 2
        + [pltpu.SemaphoreType.DMA((2,))] * 2,
        compiler_params=pltpu.CompilerParams(
            collective_id=0, has_side_effects=True, vmem_limit_bytes=50 << 20
        ),
        name="hierarchical",
    )(query_rows, key_rows, value_rows, grad_out)


def solution(mesh):
    placed = P(("grp", "seq"), None)
    return jax.shard_map(
        body, mesh=mesh, in_specs=(placed,) * 4, out_specs=(placed,) * 4, check_vma=False
    )
```
